32 devices in a mesh: blk: 4 (over y, x), dp: 8 (over z, core).
Axes of the slice: x: 2, y: 2, z: 4, core: 2. Of those that a mesh axis runs over, the one named last changes fastest.
Arguments:
- embed: bfloat16 [8192, 768], P(('blk', 'dp')), may hold values from -0.23925781 to 0.23925781
- log_scale: float32 [1], replicated, may hold values from 3 to 3.7
- bias: float32 [1], replicated, may hold values from -5.5 to -3.5
- partner_count: int32 [8192], P(('blk', 'dp')), may hold values from 1 to 4, as said below
- partner_owner: int32 [8192, 4], P(('blk', 'dp')), may hold values from 0 to 31, as said below
- partner_row: int32 [8192, 4], P(('blk', 'dp')), may hold values from 0 to 255
Outputs:
- embed_grad: bfloat16 [8192, 768], P(('blk', 'dp'))
The draws below stay inside these ranges and needn't reach their ends.
Inputs may be any that keep to these rules, and one draw needn't show every extreme that they name: `partner_count`: 4 on some row of every device. `partner_owner`: every entry names a device other than the row's own device (devices numbered index along blk times 8 plus index along dp). Among the first partner_count entries of the rows of one device, no device is named more than 34 times, and some device exactly 34 times.
All inputs are finite; a program needn't handle non-finite values.
Results may differ from the reference program's by a relative error of at most 0.0065.
Values may be sent and summed in bfloat16 or wider, within the bound.
A program may use at most 64 MiB of HBM per device.

```python
import math
import jax
import jax.numpy as jnp
from jax import lax

D = 768
ROWS_DEV = 256
KMAX = 4
ROWS = 8192
GROUP = 1024
CAP = 34
N_BLK = 4
N_DP = 8
DEVICES = 32


def partner_tables(key):
    valid_owners = DEVICES - 1

    def one_device(dev_key, device):
        keys = jax.random.split(dev_key, 5)
        level = jax.random.randint(keys[0], (), 1, KMAX + 1)
        counts = jax.random.randint(keys[1], (ROWS_DEV,), 0, KMAX + 1) % (KMAX + 1 - level) + level
        forced = jax.random.randint(keys[2], (), 0, ROWS_DEV)
        counts = jnp.where(jnp.arange(ROWS_DEV) == forced, KMAX, counts).astype(jnp.int32)
        hot = jax.random.randint(keys[3], (), 0, valid_owners)
        others = jnp.arange((valid_owners - 1) * CAP, dtype=jnp.int32) // CAP
        others = others + (others >= hot).astype(jnp.int32)
        others = jax.random.permutation(keys[4], others)
        sequence = jnp.concatenate([jnp.full((CAP,), hot, jnp.int32), others])
        starts = jnp.cumsum(counts) - counts
        positions = starts[:, None] + jnp.arange(KMAX, dtype=jnp.int32)[None, :]
        positions = jnp.minimum(positions, valid_owners * CAP - 1)
        chosen = sequence[positions]
        owners = chosen + (chosen >= device).astype(jnp.int32)
        return (counts, owners.astype(jnp.int32))
    dev_keys = jax.random.split(jax.random.fold_in(key, 17), DEVICES)
    counts, owners = jax.vmap(one_device)(dev_keys, jnp.arange(DEVICES, dtype=jnp.int32))
    return (counts.reshape(ROWS), owners.reshape(ROWS, KMAX))


def draw_partner_count(key, part):
    return partner_tables(key)[0]


def draw_partner_owner(key, part):
    return partner_tables(key)[1]


def with_ends(values, stream_key, low, high):
    spot = [jax.random.randint(jax.random.fold_in(stream_key, axis), (), 0, length) for axis, length in enumerate(values.shape)]
    main_axis = values.shape.index(max(values.shape))
    next_to = spot[:main_axis] + [(spot[main_axis] + 1) % values.shape[main_axis]] + spot[main_axis + 1:]
    return values.at[tuple(spot)].set(low).at[tuple(next_to)].set(high)


def steps_of(rng, shape, shards, smallest, high):
    gain = 1.0
    for position, shards_of in shards:
        heights = jax.random.uniform(jax.random.fold_in(jax.random.fold_in(rng, 6), position), (shards_of,), jnp.float32, smallest / len(shards), high / len(shards))
        gain = gain * jnp.repeat(jnp.exp(heights), shape[position] // shards_of).reshape((-1,) + (1,) * (len(shape) - 1 - position))
    return gain


def scatter_about(key, extent, deviation, reach, shards=(), kind=jnp.bfloat16):
    array = jax.random.normal(key, extent, jnp.float32) * deviation
    if len(shards) > 0:
        array = steps_of(key, extent, shards, -0.22, 0.18) * array
    return jnp.clip(array, min=-reach, max=reach).astype(kind)


def setup_inputs(seed: int = 0) -> dict:
    splits = jax.random.split(jax.random.key(seed), 7)
    embed = scatter_about(splits[0], (ROWS, D), 0.04, 0.23925781, ((0, 32),))
    log_scale = jnp.clip(jax.random.uniform(splits[1], (1,), jnp.float32, 3.0, 3.7), 3.0, 3.7)
    bias = jnp.clip(jax.random.uniform(splits[2], (1,), jnp.float32, -5.5, -3.5), -5.5, -3.5)
    partner_count = draw_partner_count(jax.random.fold_in(splits[6], 71), 0)
    partner_owner = draw_partner_owner(jax.random.fold_in(splits[6], 71), 0)
    partner_row = with_ends(jax.random.randint(splits[5], (ROWS, KMAX), 0, ROWS_DEV), jax.random.fold_in(splits[5], 1), 0, ROWS_DEV - 1).astype(jnp.int32)
    return dict(embed=embed, log_scale=log_scale, bias=bias, partner_count=partner_count, partner_owner=partner_owner, partner_row=partner_row)


def reference(embed, log_scale, bias, partner_count, partner_owner, partner_row):
    highest = lax.Precision.HIGHEST
    values = embed.astype(jnp.float32)
    inv_norm = lax.rsqrt(lax.optimization_barrier(jnp.mean(values * values, axis=1, keepdims=True)) + 1e-06)
    root_width = 1.0 / math.sqrt(D)
    unit_rows = (values * inv_norm * root_width).astype(jnp.bfloat16)
    logit_scale = jnp.exp(log_scale[0])
    logit_bias = bias[0]
    blocks = unit_rows.reshape(N_BLK, N_DP, ROWS_DEV, D)

    def negative(device):
        cycle_pos = device // N_DP
        group_id = device % N_DP
        group = lax.dynamic_index_in_dim(blocks, group_id, 1, keepdims=False).reshape(GROUP, D).astype(jnp.float32)
        own_rows = lax.dynamic_slice_in_dim(group, cycle_pos * ROWS_DEV, ROWS_DEV, 0)
        scores = jnp.dot(own_rows, group.T, precision=highest)
        here = cycle_pos * ROWS_DEV + jnp.arange(ROWS_DEV, dtype=jnp.int32)
        columns = jnp.arange(GROUP, dtype=jnp.int32)
        weights = jnp.where(here[:, None] == columns[None, :], jnp.float32(0.0), jax.nn.sigmoid(logit_bias + logit_scale * scores))
        weights = weights.astype(jnp.bfloat16).astype(jnp.float32)
        return 2.0 * logit_scale * jnp.dot(weights, group, precision=highest)
    neg_grad = lax.map(negative, jnp.arange(DEVICES, dtype=jnp.int32)).reshape(ROWS, D)
    global_index = (partner_owner * ROWS_DEV + partner_row).astype(jnp.int32)
    live_all = jnp.arange(KMAX, dtype=jnp.int32)[None, :] < partner_count[:, None]

    def positive(incoming, device):
        start = (device * ROWS_DEV).astype(jnp.int32)
        own_rows = lax.dynamic_slice_in_dim(unit_rows, start, ROWS_DEV, 0).astype(jnp.float32)
        index = lax.dynamic_slice_in_dim(global_index, start, ROWS_DEV, 0)
        live = lax.dynamic_slice_in_dim(live_all, start, ROWS_DEV, 0)
        partner = unit_rows[index.reshape(-1)].astype(jnp.float32).reshape(ROWS_DEV, KMAX, D)
        scores = jnp.einsum('rd,rkd->rk', own_rows, partner, precision=highest)
        weight = jnp.where(live, jax.nn.sigmoid(-(logit_bias + logit_scale * scores)), jnp.float32(0.0))
        own_term = (-logit_scale * weight[:, :, None] * partner).astype(jnp.bfloat16)
        back_term = (-logit_scale * weight[:, :, None] * own_rows[:, None, :]).astype(jnp.bfloat16)
        incoming = incoming.at[index.reshape(-1)].add(back_term.reshape(-1, D).astype(jnp.float32))
        return (incoming, lax.optimization_barrier(jnp.sum(own_term.astype(jnp.float32), axis=1)))
    incoming, own_sum = lax.scan(positive, jnp.zeros((ROWS, D), jnp.float32), jnp.arange(DEVICES, dtype=jnp.int32))
    row_grad = neg_grad + own_sum.reshape(ROWS, D) + incoming
    inner = lax.optimization_barrier(jnp.sum(values * row_grad, axis=1, keepdims=True))
    result = root_width * inv_norm * (row_grad - values * inv_norm * inv_norm * inner / D)
    return result.astype(jnp.bfloat16)
```

```python
import functools
import math

import jax
import jax.numpy as jnp
from jax import lax
from jax.experimental import pallas as pl
from jax.experimental.pallas import tpu as pltpu
from jax.sharding import PartitionSpec as P

MESH = pl.DeviceIdType.MESH


def lookup(table, index):
    value = jnp.int32(table[0])
    for k in range(1, len(table)):
        value = jnp.where(index == k, jnp.int32(table[k]), value)
    return value


def kernel(
    n_blk, n_dp, log_scale_ref, bias_ref, x_ref, theirs_ref, o_ref,
    buf, keys, acc, wanted, z_sem, right_sem, left_sem, sib_sem, recv_sem, key_send, key_recv,
):
    rows, width = x_ref.shape
    most = theirs_ref.shape[1]
    half = rows // 2
    n_all = n_blk * n_dp
    n_z = n_dp // 2
    far = n_blk // 2
    events = n_blk * n_z
    i, j = lax.axis_index("blk"), lax.axis_index("dp")
    z, c = j // 2, j % 2
    me = i * n_dp + j

    ring = [p ^ (p >> 1) for p in range(n_blk)]
    place = [ring.index(k) for k in range(n_blk)]
    pos = lookup(place, i)
    blk_at = lambda p: lookup(ring, lax.rem(p + n_blk, n_blk))
    right, left = blk_at(pos + 1), blk_at(pos - 1)
    order = []
    for a in range(n_z):
        order += sorted(range(n_z), key=lambda b: (abs(b - a), b))
    z_at = lambda t: lookup(order, z * n_z + t)
    slot = lambda bi, zz, cc: (bi * n_z + zz) * 2 + cc

    def copy(f, h, device, send, recv):
        if h is None:
            span = pl.ds(pl.multiple_of(f * rows, rows), rows)
        else:
            span = pl.ds(pl.multiple_of(f * rows + h * half, half), half)
        return pltpu.make_async_remote_copy(
            src_ref=buf.at[span], dst_ref=buf.at[span], send_sem=send, recv_sem=recv,
            device_id=device, device_id_type=MESH,
        )

    def to_right(f, h, e):
        return copy(f, h, (right, j), right_sem.at[e], recv_sem.at[f, h or 0])

    def to_left(f, h, e):
        return copy(f, h, (left, j), left_sem.at[e], recv_sem.at[f, h or 0])

    def to_sib(f, e):
        return copy(f, None, (i, z * 2 + 1 - c), sib_sem.at[e], recv_sem.at[f, 0])

    def along_z(zz, step, k):
        f = slot(i, zz, c)
        return copy(f, None, (i, (z + step) * 2 + c), z_sem.at[zz, k], recv_sem.at[f, 0])

    far_blk = blk_at(pos + far)

    def far_along_z(zz, step, k):
        f = slot(far_blk, zz, c)
        return copy(f, None, (i, (z + step) * 2 + c), z_sem.at[zz, 2 + k], recv_sem.at[f, 0])

    def reach(zz):
        return jnp.where(jnp.logical_and(zz >= 0, zz < n_z), 1, 0)

    def halves(zz):
        return jnp.logical_or(zz == z, jnp.maximum(zz - z, z - zz) > reach(z))

    def arrived(f, h):
        copy(f, h, (right, j), right_sem.at[0], recv_sem.at[f, h or 0]).wait_recv()

    def place_of(e):
        t, m = e // n_blk, e % n_blk
        t = jnp.where(m == n_blk - 1, t - 1, t)
        d = (m + 1) // 2
        return t, m, d, blk_at(jnp.where(m % 2 == 1, pos - d, pos + d)), z_at(t)

    barrier = pltpu.get_barrier_semaphore()

    @pl.loop(1, n_all)
    def _(k):
        f = lax.rem(me + k, n_all)
        pl.semaphore_signal(barrier, 1, device_id=(f // n_dp, f % n_dp), device_id_type=MESH)

    root = 1.0 / math.sqrt(width)
    x = x_ref[...].astype(jnp.float32)
    inv = lax.rsqrt(jnp.mean(x * x, axis=1, keepdims=True) + 1e-06)
    own = pl.ds(pl.multiple_of(me * rows, rows), rows)
    buf[own, :] = (x * inv * root).astype(jnp.bfloat16)
    keys[pl.ds(me, 1)] = theirs_ref[...]
    pl.semaphore_wait(barrier, n_all - 1)

    to_right(me, None, z).start()
    to_left(me, None, z).start()

    @pl.when(z < n_z - 1)
    def _():
        along_z(z, 1, 0).start()

    @pl.when(z > 0)
    def _():
        along_z(z, -1, 1).start()

    to_sib(me, z).start()

    def key_copy(src, dst, f):
        return pltpu.make_async_remote_copy(
            src_ref=src, dst_ref=dst, send_sem=key_send, recv_sem=key_recv,
            device_id=(f // n_dp, f % n_dp), device_id_type=MESH,
        )

    @pl.loop(1, n_all)
    def _(k):
        f = lax.rem(me + k, n_all)
        key_copy(theirs_ref, keys.at[pl.ds(me, 1)], f).start()

    acc[...] = jnp.zeros_like(acc)
    for k in range(most):
        wanted[k] = jnp.broadcast_to(theirs_ref[0, k : k + 1, :], (128, rows)).T
    scale = jnp.exp(jnp.full((1, 1), log_scale_ref[0], jnp.float32))
    offset = jnp.full((1, 1), bias_ref[0], jnp.float32)
    everything = keys.at[pl.ds(0, n_all - 1)]

    def compute(e):
        _, _, _, bi, zz = place_of(e)
        arrived(slot(bi, zz, 1 - c), None)
        pair = bi * n_z + zz
        start = pair * 2 * rows
        block = buf[pl.ds(pl.multiple_of(start, 2 * rows), 2 * rows), :]
        scores = lax.dot_general(
            buf[own, :], block, (((1,), (1,)), ((), ())), preferred_element_type=jnp.float32
        )
        lanes = lax.broadcasted_iota(jnp.int32, (rows, 128), 1)
        here = lax.broadcasted_iota(jnp.int32, (rows, 128), 0) + me * rows
        weights = []
        for u in range(2 * rows // 128):
            side, at = u * 128 // rows, u * 128 % rows
            columns = lanes + (start + u * 128)
            named = jnp.zeros((rows, 128), jnp.float32)
            for k in range(most):
                named += jnp.where(wanted[k] == columns, 1.0, 0.0)
            for k in range(most):
                key = keys[pair * 2 + side, k : k + 1, at : at + 128]
                named += jnp.where(key == here, 1.0, 0.0)
            power = jnp.exp(offset + scale * scores[:, u * 128 : (u + 1) * 128])
            gain = jnp.where(jnp.logical_and(zz == z, c == side), 2.0, 0.0)
            negative = jnp.where(columns == here, 0.0, gain * power)
            weights.append(((negative - named) / (1.0 + power)).astype(jnp.bfloat16))
        weight = jnp.concatenate(weights, axis=1)
        acc[...] += jnp.dot(weight, block, preferred_element_type=jnp.float32)

    @pl.loop(0, events + n_blk)
    def _(e):
        t, m, d, bi, zz = place_of(e)
        valid = jnp.logical_and(t >= 0, t < n_z)

        for step, k in ((1, 1), (-1, 0)):
            origin = z + step * (t + 1)

            @pl.when(jnp.logical_and(m == 0, jnp.logical_and(origin >= 0, origin < n_z)))
            def _():
                f = slot(i, origin, c)
                arrived(f, None)

                @pl.when(jnp.logical_and(z - step >= 0, z - step < n_z))
                def _():
                    along_z(origin, -step, k).start()

                to_right(f, None, origin).start()
                to_left(f, None, origin).start()
                to_sib(f, origin).start()

        passing = jnp.logical_and(valid, jnp.logical_and(m % 2 == 1, m < n_blk - 1))
        for parity, send in ((1, to_right), (0, to_left)):
            f = slot(blk_at(pos - d if parity else pos + d), zz, c)
            index = (2 * d - parity) * n_z + zz

            @pl.when(passing)
            def _():
                arrived(f, None)

            @pl.when(jnp.logical_and(jnp.logical_and(passing, halves(zz)), d == far - 1))
            def _():
                send(f, 1 - parity, index).start()

            if far > 2:
                @pl.when(jnp.logical_and(passing, d < far - 1))
                def _():
                    send(f, None, index).start()

            @pl.when(passing)
            def _():
                to_sib(f, index).start()

        for step, k in ((1, 1), (-1, 0)):
            origin = z + step * t
            here = jnp.logical_and(origin >= 0, origin < n_z)
            here = jnp.logical_and(here, jnp.logical_and(m == n_blk - 1, valid))
            if step < 0:
                here = jnp.logical_and(here, t > 0)

            @pl.when(here)
            def _():
                g = slot(far_blk, origin, c)

                @pl.when(halves(origin))
                def _():
                    arrived(g, 0)
                    arrived(g, 1)

                @pl.when(jnp.logical_not(halves(origin)))
                def _():
                    arrived(g, None)

                @pl.when(t + 1 <= reach(z - step))
                def _():
                    far_along_z(origin, -step, k).start()

                @pl.when(jnp.logical_and(t == 0, 1 <= reach(z + step)))
                def _():
                    far_along_z(origin, step, 1 - k).start()

                to_sib(g, (n_blk - 1) * n_z + origin).start()

        @pl.when(e == 1)
        def _():
            key_copy(everything, everything, lax.rem(me + 1, n_all)).wait()

        before = place_of(e - 1 + n_blk)[0] - 1

        @pl.when(jnp.logical_and(e > 0, jnp.logical_and(before >= 0, before < n_z)))
        def _():
            compute(e - 1)

    compute(events + n_blk - 1)

    t_acc = scale * acc[...]
    x = x_ref[...].astype(jnp.float32)
    inv = lax.rsqrt(jnp.mean(x * x, axis=1, keepdims=True) + 1e-06)
    inner = jnp.sum(x * t_acc, axis=1, keepdims=True)
    o_ref[...] = (root * inv * (t_acc - x * (inv * inv * inner / width))).astype(o_ref.dtype)

    @pl.loop(0, n_z)
    def _(zz):
        @pl.when(jnp.logical_and(zz <= z, z < n_z - 1))
        def _():
            along_z(zz, 1, 0).wait_send()

        @pl.when(jnp.logical_and(zz >= z, z > 0))
        def _():
            along_z(zz, -1, 1).wait_send()

        @pl.when(jnp.logical_and(zz <= z, z + 1 - zz <= reach(z + 1)))
        def _():
            far_along_z(zz, 1, 0).wait_send()

        @pl.when(jnp.logical_and(zz >= z, zz - z + 1 <= reach(z - 1)))
        def _():
            far_along_z(zz, -1, 1).wait_send()

    @pl.loop(0, events)
    def _(e):
        m, zz = e // n_z, e % n_z
        to_sib(me, e).wait_send()

        @pl.when(m == 0)
        def _():
            to_right(me, None, e).wait_send()
            to_left(me, None, e).wait_send()

        passing = jnp.logical_and(m > 0, m < n_blk - 1)
        for parity, send in ((1, to_right), (0, to_left)):
            mine = jnp.logical_and(passing, m % 2 == parity)

            @pl.when(jnp.logical_and(jnp.logical_and(mine, halves(zz)), (m + 1) // 2 == far - 1))
            def _():
                send(me, 0, e).wait_send()

            if far > 2:
                @pl.when(jnp.logical_and(mine, (m + 1) // 2 < far - 1))
                def _():
                    send(me, None, e).wait_send()


def plane_kernel(
    log_scale_ref, bias_ref, x_ref, count_ref, owner_ref, row_ref, o_ref,
    grp, col, grp_keys, col_keys, wanted, here, acc, back, out_sums, in_sums, mine_back, their_back, far_back,
    send_sem, recv_sem,
):
    rows, width = x_ref.shape
    most = owner_ref.shape[0]
    half = rows // 2
    n_dp = 8
    i, j = lax.axis_index("blk"), lax.axis_index("dp")
    z, c = j // 2, j % 2
    low = z < 2
    mid = jnp.logical_or(z == 1, z == 2)
    end = jnp.logical_not(mid)
    inner = jnp.where(low, z + 1, z - 1)
    outer = jnp.where(low, z - 1, z + 1)
    far = jnp.where(mid, 3 - outer, 3 - z)
    opposite = jnp.where(low, 2, 1)
    blk_of = [i, i + 1 - 2 * (i % 2), (i + 2) % 4, (i + 1 - 2 * (i % 2) + 2) % 4]
    X, Y = (blk_of[1], j), (blk_of[2], j)
    SIB = (i, z * 2 + 1 - c)
    IN, OUT = (i, inner * 2 + c), (i, outer * 2 + c)
    FAR = (i, jnp.where(mid, far, opposite) * 2 + c)
    planes = [z, inner, outer, far]
    first = jnp.where(mid, 3, 1)
    second = jnp.where(mid, 1, 3)

    def copy(src, dst, send, recv, device):
        return pltpu.make_async_remote_copy(
            src_ref=src, dst_ref=dst, send_sem=send_sem.at[send], recv_sem=recv_sem.at[recv],
            device_id=device, device_id_type=MESH,
        )

    def part(ref, slot, lo, size):
        return ref.at[slot, pl.ds(lo, size)]

    def group(slot, h, device, send, recv, source=0):
        return copy(part(grp, source, h * half, half), part(grp, slot, h * half, half), send, recv, device)

    to_x = [group(1, h, X, h, h) for h in range(2)]
    to_y = [group(2, h, Y, 2 + h, 2 + h) for h in range(2)]
    x_on = group(3, 0, Y, 4, 4, 1)
    y_on = group(3, 1, X, 5, 5, 2)
    keys_x = copy(grp_keys.at[0], grp_keys.at[1], 6, 6, X)
    keys_y = copy(grp_keys.at[0], grp_keys.at[2], 7, 7, Y)
    keys_on = copy(grp_keys.at[1], grp_keys.at[3], 8, 8, Y)

    def own_col(slot, h, lo, size, device, send, recv):
        return copy(
            part(grp, 0, h * half + lo, size), col.at[slot, h, c, pl.ds(lo, size)], send, recv, device
        )

    quarter = half // 2
    in_slot = jnp.where(mid, 1, 2)
    in_recv = jnp.where(mid, 9, 12)
    to_in = [own_col(in_slot, h, 0, half, IN, 9 + h, in_recv + h) for h in range(2)]
    in_keys = copy(grp_keys.at[0], col_keys.at[in_slot, c], 11, in_recv + 2, IN)
    to_out = [own_col(1, h, 0, half, OUT, 12 + h, 9 + h) for h in range(2)]
    out_keys = copy(grp_keys.at[0], col_keys.at[1, c], 14, 11, OUT)
    to_far = [own_col(3, 0, 0, half, FAR, 15, 15)]
    to_far += [own_col(3, 1, q * quarter, quarter, FAR, 16 + q, 16 + q) for q in range(2)]
    far_keys = copy(grp_keys.at[0], col_keys.at[3, c], 18, 18, FAR)

    def pass_on(h):
        return copy(col.at[3, h, c], col.at[3, h, c], 19 + h, 19 + h, OUT)

    keys_out = copy(col_keys.at[3, c], col_keys.at[3, c], 21, 21, OUT)

    def sib(p, h):
        return copy(col.at[p, h, c], col.at[p, h, c], 22 + p * 3 + h, 22 + p * 3 + h, SIB)

    def sib_keys(p):
        return copy(col_keys.at[p, c], col_keys.at[p, c], 22 + p * 3 + 2, 22 + p * 3 + 2, SIB)

    diag_x = copy(part(out_sums, 2, 0, half), part(in_sums, 2, 0, half), 34, 34, X)
    diag_y = copy(part(out_sums, 2, half, half), part(in_sums, 2, half, half), 35, 35, Y)
    back_x = [copy(part(out_sums, 0, h * half, half), part(in_sums, 0, h * half, half), 36 + h, 36 + h, X) for h in range(2)]
    back_y = [copy(part(out_sums, 1, h * half, half), part(in_sums, 1, h * half, half), 38 + h, 38 + h, Y) for h in range(2)]
    swap = copy(mine_back.at[1], their_back, 40, 40, SIB)
    home = copy(mine_back.at[0], far_back, 41, 41, FAR)

    barrier = pltpu.get_barrier_semaphore()
    for device in (X, Y, SIB, IN, FAR):
        pl.semaphore_signal(barrier, 1, device_id=device, device_id_type=MESH)

    @pl.when(mid)
    def _():
        pl.semaphore_signal(barrier, 1, device_id=OUT, device_id_type=MESH)

    root = 1.0 / math.sqrt(width)
    x = x_ref[...].astype(jnp.float32)
    inv = lax.rsqrt(jnp.mean(x * x, axis=1, keepdims=True) + 1e-06)
    unit = (x * inv * root).astype(jnp.bfloat16)
    grp[0] = unit
    live = lax.broadcasted_iota(jnp.int32, (most, rows), 0) < count_ref[...]
    grp_keys[0] = jnp.where(live, owner_ref[...] * rows + row_ref[...], -1)
    pl.semaphore_wait(barrier, 5 + jnp.where(mid, 1, 0))

    to_x[0].start()
    to_y[1].start()

    @pl.when(mid)
    def _():
        to_out[0].start()

    @pl.when(end)
    def _():
        to_far[0].start()

    for h in range(2):
        col[0, h, c] = unit[h * half : (h + 1) * half]
    col_keys[0, c] = grp_keys[0]
    sib(0, 0).start()
    sib(0, 1).start()
    to_x[1].start()
    to_y[0].start()

    @pl.when(mid)
    def _():
        to_out[1].start()
        out_keys.start()

    @pl.when(end)
    def _():
        to_far[1].start()
        to_far[2].start()
        far_keys.start()

    sib_keys(0).start()
    keys_x.start()
    keys_y.start()

    scale = 0.5 * jnp.exp(jnp.full((1, 1), log_scale_ref[0], jnp.float32))
    offset = 0.5 * jnp.full((1, 1), bias_ref[0], jnp.float32)

    def prepare(slot):
        base = (blk_of[slot] * n_dp + j) * rows
        here[slot] = (lax.broadcasted_iota(jnp.int32, (rows, 128), 0) + base).astype(jnp.int16)
        for k in range(most):
            wanted[slot, k] = jnp.broadcast_to(grp_keys[slot, k : k + 1, :], (128, rows)).T.astype(jnp.int16)

    def run(slots, p, h, negative=False, backward=False):
        if isinstance(p, int):
            plane = planes[p]
        else:
            plane = lookup_plane(p)
        block = col[p, h].reshape(rows, width)
        scores = [
            lax.dot_general(grp[g], block, (((1,), (1,)), ((), ())), preferred_element_type=jnp.float32)
            for g in slots
        ]
        one, zero = jnp.bfloat16(1.0), jnp.bfloat16(0.0)
        weights = []
        for n, g in enumerate(slots):
            pieces = []
            for u in range(2):
                base = ((i * n_dp) + plane * 2 + u) * rows + h * half
                lanes = lax.broadcasted_iota(jnp.int32, (1, 128), 1) + base
                columns = jnp.broadcast_to(lanes, (rows, 128)).astype(jnp.int16)
                named = jnp.zeros((rows, 128), jnp.bfloat16)
                for k in range(most):
                    named += jnp.where(wanted[g, k] == columns, one, zero)
                for k in range(most):
                    key = col_keys[p, u, k : k + 1, h * half : (h + 1) * half]
                    key = jnp.broadcast_to(key, (rows, 128)).astype(jnp.int16)
                    named += jnp.where(key == here[g], one, zero)
                t = jnp.tanh(scale * scores[n][:, u * 128 : (u + 1) * 128] + offset)
                w = (t - 1.0).astype(jnp.bfloat16) * named
                if negative:
                    away = (t + 1.0) * jnp.where(c == u, 2.0, 0.0)
                    if g == 0:
                        own = lax.broadcasted_iota(jnp.int32, (rows, 128), 0)
                        other = lax.broadcasted_iota(jnp.int32, (rows, 128), 1) + h * half
                        away = jnp.where(own == other, 0.0, away)
                    w += away.astype(jnp.bfloat16)
                pieces.append(w)
            weights.append(jnp.concatenate(pieces, axis=1))
        for n, g in enumerate(slots):
            acc[g] += jnp.dot(weights[n], block, preferred_element_type=jnp.float32)
        if backward:
            for n, g in enumerate(slots):
                back[h] += lax.dot_general(
                    weights[n], grp[g], (((0,), (0,)), ((), ())), preferred_element_type=jnp.float32
                )

    def lookup_plane(p):
        return jnp.where(p == 1, inner, jnp.where(p == 2, outer, far))

    prepare(0)
    acc[...] = jnp.zeros_like(acc)
    back[...] = jnp.zeros_like(back)
    sib(0, 0).wait_recv()
    sib(0, 1).wait_recv()
    sib_keys(0).wait_recv()
    run([0], 0, 0, negative=True)
    run([0], 0, 1, negative=True)

    to_x[0].wait_recv()
    x_on.start()
    to_y[1].wait_recv()
    y_on.start()

    @pl.when(mid)
    def _():
        to_far[0].wait_recv()
        pass_on(0).start()
        far_keys.wait_recv()
        keys_out.start()

    @pl.when(end)
    def _():
        to_out[0].wait_recv()
        out_keys.wait_recv()

    sib(first, 0).start()
    sib_keys(first).start()
    keys_x.wait_recv()
    keys_on.start()
    keys_y.wait_recv()
    prepare(1)
    prepare(2)

    @pl.when(mid)
    def _():
        to_far[1].wait_recv()

    @pl.when(end)
    def _():
        to_far[1].wait_send()

    for h in range(2):
        to_in[h].start()
    in_keys.start()
    sib(first, 0).wait_recv()
    sib_keys(first).wait_recv()
    run([0], first, 0, backward=True)

    @pl.when(mid)
    def _():
        to_far[2].wait_recv()
        pass_on(1).start()

    @pl.when(end)
    def _():
        to_out[1].wait_recv()

    sib(first, 1).start()
    to_x[1].wait_recv()
    to_y[0].wait_recv()
    run([1, 2], 0, 0, negative=True)
    run([1, 2], 0, 1, negative=True)
    run([1, 2], first, 0, backward=True)
    sib(first, 1).wait_recv()
    run([0, 1, 2], first, 1, backward=True)

    keys_on.wait_recv()
    prepare(3)
    x_on.wait_recv()
    y_on.wait_recv()
    run([3], 0, 0, negative=True)
    run([3], 0, 1, negative=True)
    run([3], first, 0, backward=True)
    run([3], first, 1, backward=True)

    def arrived(p, h):
        return own_col(p, h, 0, half, IN, 9 + h, (9 if p == 1 else 12) + h)

    def keys_arrived(p):
        return copy(grp_keys.at[0], col_keys.at[p, c], 11, 11 if p == 1 else 14, IN)

    @pl.when(mid)
    def _():
        arrived(1, 0).wait_recv()
        keys_arrived(1).wait_recv()
        arrived(2, 0).wait_recv()
        keys_arrived(2).wait_recv()
        sib(2, 0).start()
        sib_keys(2).start()

    @pl.when(end)
    def _():
        pass_on(0).wait_recv()
        keys_out.wait_recv()

    sib(second, 0).start()
    sib_keys(second).start()

    @pl.when(mid)
    def _():
        for h in range(2):
            other = back[h, pl.ds(pl.multiple_of((1 - c) * half, half), half), :]
            mine_back[1, h * half : (h + 1) * half] = other.astype(jnp.bfloat16)
        swap.start()

    sib(second, 0).wait_recv()
    sib_keys(second).wait_recv()
    run([0, 1, 2, 3], second, 0)

    @pl.when(mid)
    def _():
        sib(2, 0).wait_recv()
        sib_keys(2).wait_recv()
        run([0, 1, 2, 3], 2, 0)
        swap.wait_recv()
        for h in range(2):
            mine = back[h, pl.ds(pl.multiple_of(c * half, half), half), :]
            both = mine + their_back[h * half : (h + 1) * half].astype(jnp.float32)
            mine_back[0, h * half : (h + 1) * half] = both.astype(jnp.bfloat16)
        home.start()
        arrived(1, 1).wait_recv()
        arrived(2, 1).wait_recv()
        sib(2, 1).start()

    @pl.when(end)
    def _():
        pass_on(1).wait_recv()

    sib(second, 1).start()
    sib(second, 1).wait_recv()

    @pl.when(mid)
    def _():
        sib(2, 1).wait_recv()

    def last(slots):
        run(slots, second, 1)

        @pl.when(mid)
        def _():
            run(slots, 2, 1)

    last([3])
    out_sums[2] = acc[3].astype(jnp.bfloat16)
    diag_x.start()
    diag_y.start()
    last([1, 2])
    out_sums[0, :half] = acc[1, :half].astype(jnp.bfloat16)
    back_x[0].start()
    out_sums[1, half:] = acc[2, half:].astype(jnp.bfloat16)
    back_y[1].start()
    last([0])
    diag_x.wait_recv()
    out_sums[1, :half] = (acc[2, :half] + in_sums[2, :half].astype(jnp.float32)).astype(jnp.bfloat16)
    back_y[0].start()
    diag_y.wait_recv()
    out_sums[0, half:] = (acc[1, half:] + in_sums[2, half:].astype(jnp.float32)).astype(jnp.bfloat16)
    back_x[1].start()

    @pl.when(end)
    def _():
        home.wait_recv()
        acc[0] += far_back[...].astype(jnp.float32)

    back_x[0].wait_recv()
    back_y[1].wait_recv()
    back_y[0].wait_recv()
    back_x[1].wait_recv()
    total = acc[0] + in_sums[0].astype(jnp.float32) + in_sums[1].astype(jnp.float32)
    t_acc = scale * total
    x = x_ref[...].astype(jnp.float32)
    inv = lax.rsqrt(jnp.mean(x * x, axis=1, keepdims=True) + 1e-06)
    inner_sum = jnp.sum(x * t_acc, axis=1, keepdims=True)
    o_ref[...] = (root * inv * (t_acc - x * (inv * inv * inner_sum / width))).astype(o_ref.dtype)

    for sent in to_x + to_y + to_in + back_x + back_y:
        sent.wait_send()
    for sent in (x_on, y_on, keys_x, keys_y, keys_on, in_keys, diag_x, diag_y):
        sent.wait_send()
    for p in (0, 1, 3):
        for h in range(2):
            sib(p, h).wait_send()
        sib_keys(p).wait_send()

    @pl.when(mid)
    def _():
        for sent in to_out + [out_keys, pass_on(0), pass_on(1), keys_out, sib(2, 0), sib(2, 1), sib_keys(2), swap, home]:
            sent.wait_send()

    @pl.when(end)
    def _():
        for sent in (to_far[0], to_far[2], far_keys):
            sent.wait_send()


def plane_call(embed, log_scale, bias, partner_count, partner_owner, partner_row):
    rows, width = embed.shape
    most = partner_owner.shape[1]
    half = rows // 2
    vmem = pl.BlockSpec(memory_space=pltpu.VMEM)
    smem = pl.BlockSpec(memory_space=pltpu.SMEM)
    return pl.pallas_call(
        plane_kernel,
        out_shape=jax.ShapeDtypeStruct((rows, width), embed.dtype),
        in_specs=[smem, smem, vmem, vmem, vmem, vmem],
        out_specs=vmem,
        scratch_shapes=[
            pltpu.VMEM((4, rows, width), jnp.bfloat16),
            pltpu.VMEM((4, 2, 2, half, width), jnp.bfloat16),
            pltpu.VMEM((4, most, rows), jnp.int32),
            pltpu.VMEM((4, 2, most, rows), jnp.int32),
            pltpu.VMEM((4, most, rows, 128), jnp.int16),
            pltpu.VMEM((4, rows, 128), jnp.int16),
            pltpu.VMEM((4, rows, width), jnp.float32),
            pltpu.VMEM((2, rows, width), jnp.float32),
            pltpu.VMEM((3, rows, width), jnp.bfloat16),
            pltpu.VMEM((3, rows, width), jnp.bfloat16),
            pltpu.VMEM((2, rows, width), jnp.bfloat16),
            pltpu.VMEM((rows, width), jnp.bfloat16),
            pltpu.VMEM((rows, width), jnp.bfloat16),
            pltpu.SemaphoreType.DMA((42,)),
            pltpu.SemaphoreType.DMA((42,)),
        ],
        compiler_params=pltpu.CompilerParams(
            collective_id=0, has_side_effects=True, vmem_limit_bytes=60 * 1024 * 1024
        ),
    )(log_scale, bias, embed, partner_count.reshape(1, rows), partner_owner.T, partner_row.T)


def body(n_blk, n_dp, embed, log_scale, bias, partner_count, partner_owner, partner_row):
    rows, width = embed.shape
    most = partner_owner.shape[1]
    if (n_blk, n_dp, rows) == (4, 8, 256):
        return plane_call(embed, log_scale, bias, partner_count, partner_owner, partner_row)
    n_all = n_blk * n_dp
    events = n_all // 2
    live = jnp.arange(most, dtype=jnp.int32)[:, None] < partner_count[None, :]
    theirs = jnp.where(live, partner_owner.T * rows + partner_row.T, -1).reshape(1, most, rows)
    vmem = pl.BlockSpec(memory_space=pltpu.VMEM)
    smem = pl.BlockSpec(memory_space=pltpu.SMEM)
    return pl.pallas_call(
        functools.partial(kernel, n_blk, n_dp),
        out_shape=jax.ShapeDtypeStruct((rows, width), embed.dtype),
        in_specs=[smem, smem, vmem, vmem],
        out_specs=vmem,
        scratch_shapes=[
            pltpu.VMEM((n_all * rows, width), jnp.bfloat16),
            pltpu.VMEM((n_all, most, rows), jnp.int32),
            pltpu.VMEM((rows, width), jnp.float32),
            pltpu.VMEM((most, rows, 128), jnp.int32),
            pltpu.SemaphoreType.DMA((n_dp // 2, 4)),
            pltpu.SemaphoreType.DMA((events,)),
            pltpu.SemaphoreType.DMA((events,)),
            pltpu.SemaphoreType.DMA((events,)),
            pltpu.SemaphoreType.DMA((n_all, 2)),
            pltpu.SemaphoreType.DMA,
            pltpu.SemaphoreType.DMA,
        ],
        compiler_params=pltpu.CompilerParams(
            collective_id=0, has_side_effects=True, vmem_limit_bytes=60 * 1024 * 1024
        ),
    )(log_scale, bias, embed, theirs)


def solution(mesh):
    return jax.shard_map(
        functools.partial(body, mesh.shape["blk"], mesh.shape["dp"]),
        mesh=mesh,
        in_specs=(
            P(("blk", "dp"), None),
            P(),
            P(),
            P(("blk", "dp")),
            P(("blk", "dp"), None),
            P(("blk", "dp"), None),
        ),
        out_specs=P(("blk", "dp"), None),
        check_vma=False,
    )
```

```python
import functools
import math

import jax
import jax.numpy as jnp
from jax import lax
from jax.experimental import pallas as pl
from jax.experimental.pallas import tpu as pltpu
from jax.sharding import PartitionSpec as P

MESH = pl.DeviceIdType.MESH


def lookup(table, index):
    value = jnp.int32(table[0])
    for k in range(1, len(table)):
        value = jnp.where(index == k, jnp.int32(table[k]), value)
    return value


def kernel(
    n_blk, n_dp, log_scale_ref, bias_ref, x_ref, theirs_ref, o_ref,
    buf, keys, acc, wanted, z_sem, right_sem, left_sem, sib_sem, recv_sem, key_send, key_recv,
):
    rows, width = x_ref.shape
    most = theirs_ref.shape[1]
    half = rows // 2
    n_all = n_blk * n_dp
    n_z = n_dp // 2
    far = n_blk // 2
    events = n_blk * n_z
    i, j = lax.axis_index("blk"), lax.axis_index("dp")
    z, c = j // 2, j % 2
    me = i * n_dp + j

    ring = [p ^ (p >> 1) for p in range(n_blk)]
    place = [ring.index(k) for k in range(n_blk)]
    pos = lookup(place, i)
    blk_at = lambda p: lookup(ring, lax.rem(p + n_blk, n_blk))
    right, left = blk_at(pos + 1), blk_at(pos - 1)
    order = []
    for a in range(n_z):
        order += sorted(range(n_z), key=lambda b: (abs(b - a), b))
    z_at = lambda t: lookup(order, z * n_z + t)
    slot = lambda bi, zz, cc: (bi * n_z + zz) * 2 + cc

    def copy(f, h, device, send, recv):
        if h is None:
            span = pl.ds(pl.multiple_of(f * rows, rows), rows)
        else:
            span = pl.ds(pl.multiple_of(f * rows + h * half, half), half)
        return pltpu.make_async_remote_copy(
            src_ref=buf.at[span], dst_ref=buf.at[span], send_sem=send, recv_sem=recv,
            device_id=device, device_id_type=MESH,
        )

    def to_right(f, h, e):
        return copy(f, h, (right, j), right_sem.at[e], recv_sem.at[f, h or 0])

    def to_left(f, h, e):
        return copy(f, h, (left, j), left_sem.at[e], recv_sem.at[f, h or 0])

    def to_sib(f, e):
        return copy(f, None, (i, z * 2 + 1 - c), sib_sem.at[e], recv_sem.at[f, 0])

    def along_z(zz, step, k):
        f = slot(i, zz, c)
        return copy(f, None, (i, (z + step) * 2 + c), z_sem.at[zz, k], recv_sem.at[f, 0])

    far_blk = blk_at(pos + far)

    def far_along_z(zz, step, k):
        f = slot(far_blk, zz, c)
        return copy(f, None, (i, (z + step) * 2 + c), z_sem.at[zz, 2 + k], recv_sem.at[f, 0])

    def reach(zz):
        return jnp.where(jnp.logical_and(zz >= 0, zz < n_z), 1, 0)

    def halves(zz):
        return jnp.logical_or(zz == z, jnp.maximum(zz - z, z - zz) > reach(z))

    def arrived(f, h):
        copy(f, h, (right, j), right_sem.at[0], recv_sem.at[f, h or 0]).wait_recv()

    def place_of(e):
        t, m = e // n_blk, e % n_blk
        t = jnp.where(m == n_blk - 1, t - 1, t)
        d = (m + 1) // 2
        return t, m, d, blk_at(jnp.where(m % 2 == 1, pos - d, pos + d)), z_at(t)

    barrier = pltpu.get_barrier_semaphore()

    @pl.loop(1, n_all)
    def _(k):
        f = lax.rem(me + k, n_all)
        pl.semaphore_signal(barrier, 1, device_id=(f // n_dp, f % n_dp), device_id_type=MESH)

    root = 1.0 / math.sqrt(width)
    x = x_ref[...].astype(jnp.float32)
    inv = lax.rsqrt(jnp.mean(x * x, axis=1, keepdims=True) + 1e-06)
    own = pl.ds(pl.multiple_of(me * rows, rows), rows)
    buf[own, :] = (x * inv * root).astype(jnp.bfloat16)
    keys[pl.ds(me, 1)] = theirs_ref[...]
    pl.semaphore_wait(barrier, n_all - 1)

    to_right(me, None, z).start()
    to_left(me, None, z).start()

    @pl.when(z < n_z - 1)
    def _():
        along_z(z, 1, 0).start()

    @pl.when(z > 0)
    def _():
        along_z(z, -1, 1).start()

    to_sib(me, z).start()

    def key_copy(src, dst, f):
        return pltpu.make_async_remote_copy(
            src_ref=src, dst_ref=dst, send_sem=key_send, recv_sem=key_recv,
            device_id=(f // n_dp, f % n_dp), device_id_type=MESH,
        )

    @pl.loop(1, n_all)
    def _(k):
        f = lax.rem(me + k, n_all)
        key_copy(theirs_ref, keys.at[pl.ds(me, 1)], f).start()

    acc[...] = jnp.zeros_like(acc)
    for k in range(most):
        wanted[k] = jnp.broadcast_to(theirs_ref[0, k : k + 1, :], (128, rows)).T
    scale = jnp.exp(jnp.full((1, 1), log_scale_ref[0], jnp.float32))
    offset = jnp.full((1, 1), bias_ref[0], jnp.float32)
    everything = keys.at[pl.ds(0, n_all - 1)]

    def compute(e):
        _, _, _, bi, zz = place_of(e)
        arrived(slot(bi, zz, 1 - c), None)
        pair = bi * n_z + zz
        start = pair * 2 * rows
        block = buf[pl.ds(pl.multiple_of(start, 2 * rows), 2 * rows), :]
        scores = lax.dot_general(
            buf[own, :], block, (((1,), (1,)), ((), ())), preferred_element_type=jnp.float32
        )
        lanes = lax.broadcasted_iota(jnp.int32, (rows, 128), 1)
        here = lax.broadcasted_iota(jnp.int32, (rows, 128), 0) + me * rows
        weights = []
        for u in range(2 * rows // 128):
            side, at = u * 128 // rows, u * 128 % rows
            columns = lanes + (start + u * 128)
            named = jnp.zeros((rows, 128), jnp.float32)
            for k in range(most):
                named += jnp.where(wanted[k] == columns, 1.0, 0.0)
            for k in range(most):
                key = keys[pair * 2 + side, k : k + 1, at : at + 128]
                named += jnp.where(key == here, 1.0, 0.0)
            power = jnp.exp(offset + scale * scores[:, u * 128 : (u + 1) * 128])
            gain = jnp.where(jnp.logical_and(zz == z, c == side), 2.0, 0.0)
            negative = jnp.where(columns == here, 0.0, gain * power)
            weights.append(((negative - named) / (1.0 + power)).astype(jnp.bfloat16))
        weight = jnp.concatenate(weights, axis=1)
        acc[...] += jnp.dot(weight, block, preferred_element_type=jnp.float32)

    @pl.loop(0, events + n_blk)
    def _(e):
        t, m, d, bi, zz = place_of(e)
        valid = jnp.logical_and(t >= 0, t < n_z)

        for step, k in ((1, 1), (-1, 0)):
            origin = z + step * (t + 1)

            @pl.when(jnp.logical_and(m == 0, jnp.logical_and(origin >= 0, origin < n_z)))
            def _():
                f = slot(i, origin, c)
                arrived(f, None)

                @pl.when(jnp.logical_and(z - step >= 0, z - step < n_z))
                def _():
                    along_z(origin, -step, k).start()

                to_right(f, None, origin).start()
                to_left(f, None, origin).start()
                to_sib(f, origin).start()

        passing = jnp.logical_and(valid, jnp.logical_and(m % 2 == 1, m < n_blk - 1))
        for parity, send in ((1, to_right), (0, to_left)):
            f = slot(blk_at(pos - d if parity else pos + d), zz, c)
            index = (2 * d - parity) * n_z + zz

            @pl.when(passing)
            def _():
                arrived(f, None)

            @pl.when(jnp.logical_and(jnp.logical_and(passing, halves(zz)), d == far - 1))
            def _():
                send(f, 1 - parity, index).start()

            if far > 2:
                @pl.when(jnp.logical_and(passing, d < far - 1))
                def _():
                    send(f, None, index).start()

            @pl.when(passing)
            def _():
                to_sib(f, index).start()

        for step, k in ((1, 1), (-1, 0)):
            origin = z + step * t
            here = jnp.logical_and(origin >= 0, origin < n_z)
            here = jnp.logical_and(here, jnp.logical_and(m == n_blk - 1, valid))
            if step < 0:
                here = jnp.logical_and(here, t > 0)

            @pl.when(here)
            def _():
                g = slot(far_blk, origin, c)

                @pl.when(halves(origin))
                def _():
                    arrived(g, 0)
                    arrived(g, 1)

                @pl.when(jnp.logical_not(halves(origin)))
                def _():
                    arrived(g, None)

                @pl.when(t + 1 <= reach(z - step))
                def _():
                    far_along_z(origin, -step, k).start()

                @pl.when(jnp.logical_and(t == 0, 1 <= reach(z + step)))
                def _():
                    far_along_z(origin, step, 1 - k).start()

                to_sib(g, (n_blk - 1) * n_z + origin).start()

        @pl.when(e == 1)
        def _():
            key_copy(everything, everything, lax.rem(me + 1, n_all)).wait()

        before = place_of(e - 1 + n_blk)[0] - 1

        @pl.when(jnp.logical_and(e > 0, jnp.logical_and(before >= 0, before < n_z)))
        def _():
            compute(e - 1)

    compute(events + n_blk - 1)

    t_acc = scale * acc[...]
    x = x_ref[...].astype(jnp.float32)
    inv = lax.rsqrt(jnp.mean(x * x, axis=1, keepdims=True) + 1e-06)
    inner = jnp.sum(x * t_acc, axis=1, keepdims=True)
    o_ref[...] = (root * inv * (t_acc - x * (inv * inv * inner / width))).astype(o_ref.dtype)

    @pl.loop(0, n_z)
    def _(zz):
        @pl.when(jnp.logical_and(zz <= z, z < n_z - 1))
        def _():
            along_z(zz, 1, 0).wait_send()

        @pl.when(jnp.logical_and(zz >= z, z > 0))
        def _():
            along_z(zz, -1, 1).wait_send()

        @pl.when(jnp.logical_and(zz <= z, z + 1 - zz <= reach(z + 1)))
        def _():
            far_along_z(zz, 1, 0).wait_send()

        @pl.when(jnp.logical_and(zz >= z, zz - z + 1 <= reach(z - 1)))
        def _():
            far_along_z(zz, -1, 1).wait_send()

    @pl.loop(0, events)
    def _(e):
        m, zz = e // n_z, e % n_z
        to_sib(me, e).wait_send()

        @pl.when(m == 0)
        def _():
            to_right(me, None, e).wait_send()
            to_left(me, None, e).wait_send()

        passing = jnp.logical_and(m > 0, m < n_blk - 1)
        for parity, send in ((1, to_right), (0, to_left)):
            mine = jnp.logical_and(passing, m % 2 == parity)

            @pl.when(jnp.logical_and(jnp.logical_and(mine, halves(zz)), (m + 1) // 2 == far - 1))
            def _():
                send(me, 0, e).wait_send()

            if far > 2:
                @pl.when(jnp.logical_and(mine, (m + 1) // 2 < far - 1))
                def _():
                    send(me, None, e).wait_send()


def plane_kernel(
    log_scale_hbm, bias_hbm, x_hbm, count_hbm, owner_hbm, row_hbm, o_ref,
    log_scale_ref, bias_ref, x_ref, count_ref, owner_ref, row_ref, grp, col, grp_keys, col_keys, wanted, here, acc, back, out_sums, in_sums, mine_back, their_back, far_back,
    send_sem, recv_sem, load_sem,
):
    rows, width = x_ref.shape
    most = owner_ref.shape[0]
    loads = []
    for source, target in (
        (x_hbm, x_ref), (count_hbm, count_ref), (owner_hbm, owner_ref), (row_hbm, row_ref),
        (log_scale_hbm, log_scale_ref), (bias_hbm, bias_ref),
    ):
        loads.append(pltpu.make_async_copy(source, target, load_sem.at[len(loads)]))
        loads[-1].start()
    half = rows // 2
    n_dp = 8
    i, j = lax.axis_index("blk"), lax.axis_index("dp")
    z, c = j // 2, j % 2
    low = z < 2
    mid = jnp.logical_or(z == 1, z == 2)
    end = jnp.logical_not(mid)
    inner = jnp.where(low, z + 1, z - 1)
    outer = jnp.where(low, z - 1, z + 1)
    far = jnp.where(mid, 3 - outer, 3 - z)
    opposite = jnp.where(low, 2, 1)
    blk_of = [i, i + 1 - 2 * (i % 2), (i + 2) % 4, (i + 1 - 2 * (i % 2) + 2) % 4]
    X, Y = (blk_of[1], j), (blk_of[2], j)
    SIB = (i, z * 2 + 1 - c)
    IN, OUT = (i, inner * 2 + c), (i, outer * 2 + c)
    FAR = (i, jnp.where(mid, far, opposite) * 2 + c)
    planes = [z, inner, outer, far]
    first = jnp.where(mid, 3, 1)
    second = jnp.where(mid, 1, 3)

    def copy(src, dst, send, recv, device):
        return pltpu.make_async_remote_copy(
            src_ref=src, dst_ref=dst, send_sem=send_sem.at[send], recv_sem=recv_sem.at[recv],
            device_id=device, device_id_type=MESH,
        )

    def part(ref, slot, lo, size):
        return ref.at[slot, pl.ds(lo, size)]

    def group(slot, h, device, send, recv, source=0):
        return copy(part(grp, source, h * half, half), part(grp, slot, h * half, half), send, recv, device)

    to_x = [group(1, h, X, h, h) for h in range(2)]
    to_y = [group(2, h, Y, 2 + h, 2 + h) for h in range(2)]
    x_on = group(3, 0, Y, 4, 4, 1)
    y_on = group(3, 1, X, 5, 5, 2)
    keys_x = copy(grp_keys.at[0], grp_keys.at[1], 6, 6, X)
    keys_y = copy(grp_keys.at[0], grp_keys.at[2], 7, 7, Y)
    keys_on = copy(grp_keys.at[1], grp_keys.at[3], 8, 8, Y)

    def own_col(slot, h, lo, size, device, send, recv):
        return copy(
            part(grp, 0, h * half + lo, size), col.at[slot, h, c, pl.ds(lo, size)], send, recv, device
        )

    quarter = half // 2
    in_slot = jnp.where(mid, 1, 2)
    in_recv = jnp.where(mid, 9, 12)
    to_in = [own_col(in_slot, h, 0, half, IN, 9 + h, in_recv + h) for h in range(2)]
    in_keys = copy(grp_keys.at[0], col_keys.at[in_slot, c], 11, in_recv + 2, IN)
    to_out = [own_col(1, h, 0, half, OUT, 12 + h, 9 + h) for h in range(2)]
    out_keys = copy(grp_keys.at[0], col_keys.at[1, c], 14, 11, OUT)
    to_far = [own_col(3, 0, 0, half, FAR, 15, 15)]
    to_far += [own_col(3, 1, q * quarter, quarter, FAR, 16 + q, 16 + q) for q in range(2)]
    far_keys = copy(grp_keys.at[0], col_keys.at[3, c], 18, 18, FAR)

    def pass_on(h):
        return copy(col.at[3, h, c], col.at[3, h, c], 19 + h, 19 + h, OUT)

    keys_out = copy(col_keys.at[3, c], col_keys.at[3, c], 21, 21, OUT)

    def sib(p, h):
        return copy(col.at[p, h, c], col.at[p, h, c], 22 + p * 3 + h, 22 + p * 3 + h, SIB)

    def sib_keys(p):
        return copy(col_keys.at[p, c], col_keys.at[p, c], 22 + p * 3 + 2, 22 + p * 3 + 2, SIB)

    diag_x = copy(part(out_sums, 2, 0, half), part(in_sums, 2, 0, half), 34, 34, X)
    diag_y = copy(part(out_sums, 2, half, half), part(in_sums, 2, half, half), 35, 35, Y)
    back_x = [copy(part(out_sums, 0, h * half, half), part(in_sums, 0, h * half, half), 36 + h, 36 + h, X) for h in range(2)]
    back_y = [copy(part(out_sums, 1, h * half, half), part(in_sums, 1, h * half, half), 38 + h, 38 + h, Y) for h in range(2)]
    swap = copy(mine_back.at[1], their_back, 40, 40, SIB)
    home = copy(mine_back.at[0], far_back, 41, 41, FAR)

    barrier = pltpu.get_barrier_semaphore()
    for device in (X, Y, SIB, IN, FAR):
        pl.semaphore_signal(barrier, 1, device_id=device, device_id_type=MESH)

    @pl.when(mid)
    def _():
        pl.semaphore_signal(barrier, 1, device_id=OUT, device_id_type=MESH)

    loads[0].wait()
    root = 1.0 / math.sqrt(width)
    x = x_ref[...].astype(jnp.float32)
    inv = lax.rsqrt(jnp.mean(x * x, axis=1, keepdims=True) + 1e-06)
    unit = (x * inv * root).astype(jnp.bfloat16)
    grp[0] = unit
    for load in loads[1:]:
        load.wait()
    live = lax.broadcasted_iota(jnp.int32, (most, rows), 0) < count_ref[...]
    grp_keys[0] = jnp.where(live, owner_ref[...] * rows + row_ref[...], -1)
    pl.semaphore_wait(barrier, 5 + jnp.where(mid, 1, 0))

    to_x[0].start()
    to_y[1].start()

    @pl.when(mid)
    def _():
        to_out[0].start()

    @pl.when(end)
    def _():
        to_far[0].start()

    for h in range(2):
        col[0, h, c] = unit[h * half : (h + 1) * half]
    col_keys[0, c] = grp_keys[0]
    sib(0, 0).start()
    sib(0, 1).start()
    to_x[1].start()
    to_y[0].start()

    @pl.when(mid)
    def _():
        to_out[1].start()
        out_keys.start()

    @pl.when(end)
    def _():
        to_far[1].start()
        to_far[2].start()
        far_keys.start()

    sib_keys(0).start()
    keys_x.start()
    keys_y.start()

    scale = 0.5 * jnp.exp(jnp.full((1, 1), log_scale_ref[0], jnp.float32))
    offset = 0.5 * jnp.full((1, 1), bias_ref[0], jnp.float32)

    def prepare(slot):
        base = (blk_of[slot] * n_dp + j) * rows
        here[slot] = (lax.broadcasted_iota(jnp.int32, (rows, 128), 0) + base).astype(jnp.int16)
        for k in range(most):
            wanted[slot, k] = jnp.broadcast_to(grp_keys[slot, k : k + 1, :], (128, rows)).T.astype(jnp.int16)

    def run(slots, p, h, negative=False, backward=False):
        if isinstance(p, int):
            plane = planes[p]
        else:
            plane = lookup_plane(p)
        block = col[p, h].reshape(rows, width)
        spans = [(g, 0, rows) if isinstance(g, int) else (g[0], g[1] * half, half) for g in slots]
        scores = [
            lax.dot_general(
                grp[g, lo : lo + size], block, (((1,), (1,)), ((), ())), preferred_element_type=jnp.float32
            )
            for g, lo, size in spans
        ]
        one, zero = jnp.bfloat16(1.0), jnp.bfloat16(0.0)
        weights = []
        for n, (g, lo, size) in enumerate(spans):
            pieces = []
            for u in range(2):
                base = ((i * n_dp) + plane * 2 + u) * rows + h * half
                lanes = lax.broadcasted_iota(jnp.int32, (1, 128), 1) + base
                columns = jnp.broadcast_to(lanes, (size, 128)).astype(jnp.int16)
                named = jnp.zeros((size, 128), jnp.bfloat16)
                for k in range(most):
                    named += jnp.where(wanted[g, k, lo : lo + size] == columns, one, zero)
                for k in range(most):
                    key = col_keys[p, u, k : k + 1, h * half : (h + 1) * half]
                    key = jnp.broadcast_to(key, (size, 128)).astype(jnp.int16)
                    named += jnp.where(key == here[g, lo : lo + size], one, zero)
                t = jnp.tanh(scale * scores[n][:, u * 128 : (u + 1) * 128] + offset)
                w = (t - 1.0).astype(jnp.bfloat16) * named
                if negative:
                    away = (t + 1.0) * jnp.where(c == u, 2.0, 0.0)
                    if g == 0:
                        own = lax.broadcasted_iota(jnp.int32, (size, 128), 0) + lo
                        other = lax.broadcasted_iota(jnp.int32, (size, 128), 1) + h * half
                        away = jnp.where(own == other, 0.0, away)
                    w += away.astype(jnp.bfloat16)
                pieces.append(w)
            weights.append(jnp.concatenate(pieces, axis=1))
        for n, (g, lo, size) in enumerate(spans):
            acc[g, lo : lo + size] += jnp.dot(weights[n], block, preferred_element_type=jnp.float32)
        if backward:
            for n, (g, lo, size) in enumerate(spans):
                back[h] += lax.dot_general(
                    weights[n], grp[g, lo : lo + size], (((0,), (0,)), ((), ())),
                    preferred_element_type=jnp.float32,
                )

    early, late = [(1, 0), (2, 1)], [(1, 1), (2, 0)]

    def lookup_plane(p):
        return jnp.where(p == 1, inner, jnp.where(p == 2, outer, far))

    prepare(0)
    acc[...] = jnp.zeros_like(acc)
    back[...] = jnp.zeros_like(back)
    sib(0, 0).wait_recv()
    sib(0, 1).wait_recv()
    sib_keys(0).wait_recv()
    run([0], 0, 0, negative=True)
    run([0], 0, 1, negative=True)

    to_x[0].wait_recv()
    x_on.start()
    to_y[1].wait_recv()
    y_on.start()

    @pl.when(mid)
    def _():
        to_far[0].wait_recv()
        pass_on(0).start()
        far_keys.wait_recv()
        keys_out.start()

    @pl.when(end)
    def _():
        to_out[0].wait_recv()
        out_keys.wait_recv()

    sib(first, 0).start()
    sib_keys(first).start()
    keys_x.wait_recv()
    keys_on.start()
    keys_y.wait_recv()
    prepare(1)
    prepare(2)
    run(early, 0, 0, negative=True)

    @pl.when(mid)
    def _():
        to_far[1].wait_recv()

    @pl.when(end)
    def _():
        to_far[1].wait_send()

    for h in range(2):
        to_in[h].start()
    in_keys.start()
    run(early, 0, 1, negative=True)
    sib(first, 0).wait_recv()
    sib_keys(first).wait_recv()
    run([0] + early, first, 0, backward=True)

    @pl.when(mid)
    def _():
        to_far[2].wait_recv()
        pass_on(1).start()

    @pl.when(end)
    def _():
        to_out[1].wait_recv()

    sib(first, 1).start()
    to_x[1].wait_recv()
    to_y[0].wait_recv()
    run(late, 0, 0, negative=True)
    run(late, 0, 1, negative=True)
    run(late, first, 0, backward=True)
    keys_on.wait_recv()
    prepare(3)
    sib(first, 1).wait_recv()
    run([0, 1, 2], first, 1, backward=True)

    def arrived(p, h):
        return own_col(p, h, 0, half, IN, 9 + h, (9 if p == 1 else 12) + h)

    def keys_arrived(p):
        return copy(grp_keys.at[0], col_keys.at[p, c], 11, 11 if p == 1 else 14, IN)

    @pl.when(mid)
    def _():
        for p in (1, 2):
            arrived(p, 0).wait_recv()
            sib(p, 0).start()
            keys_arrived(p).wait_recv()
            sib_keys(p).start()

    @pl.when(end)
    def _():
        pass_on(0).wait_recv()
        sib(3, 0).start()
        keys_out.wait_recv()
        sib_keys(3).start()

    x_on.wait_recv()
    y_on.wait_recv()
    run([3], first, 0, backward=True)
    run([3], first, 1, backward=True)

    def diagonal_back():
        out_sums[2] = acc[3].astype(jnp.bfloat16)
        diag_x.start()
        diag_y.start()

    @pl.when(mid)
    def _():
        for h in range(2):
            other = back[h, pl.ds(pl.multiple_of((1 - c) * half, half), half), :]
            mine_back[1, h * half : (h + 1) * half] = other.astype(jnp.bfloat16)
        swap.start()
        for p in (1, 2):
            arrived(p, 1).wait_recv()
            sib(p, 1).start()
        for p in (1, 2):
            sib(p, 0).wait_recv()
            sib_keys(p).wait_recv()
        run([3], 0, 0, negative=True)
        run([3], 0, 1, negative=True)
        run([3], 1, 0)
        run([3], 2, 0)
        swap.wait_recv()
        for h in range(2):
            mine = back[h, pl.ds(pl.multiple_of(c * half, half), half), :]
            both = mine + their_back[h * half : (h + 1) * half].astype(jnp.float32)
            mine_back[0, h * half : (h + 1) * half] = both.astype(jnp.bfloat16)
        home.start()
        for p in (1, 2):
            sib(p, 1).wait_recv()
        run([3], 1, 1)
        run([3], 2, 1)
        diagonal_back()
        for h in range(2):
            run(early, 1, h)
            run(early, 2, h)

    @pl.when(end)
    def _():
        pass_on(1).wait_recv()
        sib(3, 1).start()
        sib(3, 0).wait_recv()
        sib_keys(3).wait_recv()
        run([3], 0, 0, negative=True)
        run([3], 0, 1, negative=True)
        run([3], 3, 0)
        sib(3, 1).wait_recv()
        run([3], 3, 1)
        diagonal_back()
        run(early, 3, 0)
        run(early, 3, 1)

    out_sums[0, :half] = acc[1, :half].astype(jnp.bfloat16)
    back_x[0].start()
    out_sums[1, half:] = acc[2, half:].astype(jnp.bfloat16)
    back_y[1].start()

    @pl.when(mid)
    def _():
        for h in range(2):
            run(late + [0], 1, h)
            run(late + [0], 2, h)

    @pl.when(end)
    def _():
        run(late + [0], 3, 0)
        run(late + [0], 3, 1)

    diag_x.wait_recv()
    out_sums[1, :half] = (acc[2, :half] + in_sums[2, :half].astype(jnp.float32)).astype(jnp.bfloat16)
    back_y[0].start()
    diag_y.wait_recv()
    out_sums[0, half:] = (acc[1, half:] + in_sums[2, half:].astype(jnp.float32)).astype(jnp.bfloat16)
    back_x[1].start()

    back_x[0].wait_recv()
    acc[0, :half] += in_sums[0, :half].astype(jnp.float32)
    back_y[1].wait_recv()
    acc[0, half:] += in_sums[1, half:].astype(jnp.float32)

    @pl.when(end)
    def _():
        home.wait_recv()
        acc[0] += far_back[...].astype(jnp.float32)

    back_y[0].wait_recv()
    o_ref[:half] = scale * (acc[0, :half] + in_sums[1, :half].astype(jnp.float32))
    back_x[1].wait_recv()
    o_ref[half:] = scale * (acc[0, half:] + in_sums[0, half:].astype(jnp.float32))

    for sent in to_x + to_y + to_in + back_x + back_y:
        sent.wait_send()
    for sent in (x_on, y_on, keys_x, keys_y, keys_on, in_keys, diag_x, diag_y):
        sent.wait_send()
    for p in (0, 1, 3):
        for h in range(2):
            sib(p, h).wait_send()
        sib_keys(p).wait_send()

    @pl.when(mid)
    def _():
        for sent in to_out + [out_keys, pass_on(0), pass_on(1), keys_out, sib(2, 0), sib(2, 1), sib_keys(2), swap, home]:
            sent.wait_send()

    @pl.when(end)
    def _():
        for sent in (to_far[0], to_far[2], far_keys):
            sent.wait_send()


def finish_kernel(x_ref, t_acc_ref, o_ref):
    width = x_ref.shape[1]
    root = 1.0 / math.sqrt(width)
    t_acc = t_acc_ref[...]
    x = x_ref[...].astype(jnp.float32)
    inv = lax.rsqrt(jnp.mean(x * x, axis=1, keepdims=True) + 1e-06)
    inner = jnp.sum(x * t_acc, axis=1, keepdims=True)
    o_ref[...] = (root * inv * (t_acc - x * (inv * inv * inner / width))).astype(o_ref.dtype)


def plane_call(embed, log_scale, bias, partner_count, partner_owner, partner_row):
    rows, width = embed.shape
    most = partner_owner.shape[1]
    half = rows // 2
    vmem = pl.BlockSpec(memory_space=pltpu.VMEM)
    hbm = pl.BlockSpec(memory_space=pltpu.HBM)
    t_acc = pl.pallas_call(
        plane_kernel,
        out_shape=jax.ShapeDtypeStruct((rows, width), jnp.float32),
        in_specs=[hbm] * 6,
        out_specs=vmem,
        scratch_shapes=[
            pltpu.SMEM((1,), jnp.float32),
            pltpu.SMEM((1,), jnp.float32),
            pltpu.VMEM((rows, width), embed.dtype),
            pltpu.VMEM((1, rows), jnp.int32),
            pltpu.VMEM((most, rows), jnp.int32),
            pltpu.VMEM((most, rows), jnp.int32),
            pltpu.VMEM((4, rows, width), jnp.bfloat16),
            pltpu.VMEM((4, 2, 2, half, width), jnp.bfloat16),
            pltpu.VMEM((4, most, rows), jnp.int32),
            pltpu.VMEM((4, 2, most, rows), jnp.int32),
            pltpu.VMEM((4, most, rows, 128), jnp.int16),
            pltpu.VMEM((4, rows, 128), jnp.int16),
            pltpu.VMEM((4, rows, width), jnp.float32),
            pltpu.VMEM((2, rows, width), jnp.float32),
            pltpu.VMEM((3, rows, width), jnp.bfloat16),
            pltpu.VMEM((3, rows, width), jnp.bfloat16),
            pltpu.VMEM((2, rows, width), jnp.bfloat16),
            pltpu.VMEM((rows, width), jnp.bfloat16),
            pltpu.VMEM((rows, width), jnp.bfloat16),
            pltpu.SemaphoreType.DMA((42,)),
            pltpu.SemaphoreType.DMA((42,)),
            pltpu.SemaphoreType.DMA((6,)),
        ],
        compiler_params=pltpu.CompilerParams(
            collective_id=0, has_side_effects=True, vmem_limit_bytes=28 * 1024 * 1024
        ),
    )(log_scale, bias, embed, partner_count.reshape(1, rows), partner_owner.T, partner_row.T)
    return pl.pallas_call(
        finish_kernel,
        out_shape=jax.ShapeDtypeStruct((rows, width), embed.dtype),
        in_specs=[vmem, vmem],
        out_specs=vmem,
        compiler_params=pltpu.CompilerParams(vmem_limit_bytes=8 * 1024 * 1024),
    )(embed, t_acc)


def body(n_blk, n_dp, embed, log_scale, bias, partner_count, partner_owner, partner_row):
    rows, width = embed.shape
    most = partner_owner.shape[1]
    if (n_blk, n_dp, rows) == (4, 8, 256):
        return plane_call(embed, log_scale, bias, partner_count, partner_owner, partner_row)
    n_all = n_blk * n_dp
    events = n_all // 2
    live = jnp.arange(most, dtype=jnp.int32)[:, None] < partner_count[None, :]
    theirs = jnp.where(live, partner_owner.T * rows + partner_row.T, -1).reshape(1, most, rows)
    vmem = pl.BlockSpec(memory_space=pltpu.VMEM)
    smem = pl.BlockSpec(memory_space=pltpu.SMEM)
    return pl.pallas_call(
        functools.partial(kernel, n_blk, n_dp),
        out_shape=jax.ShapeDtypeStruct((rows, width), embed.dtype),
        in_specs=[smem, smem, vmem, vmem],
        out_specs=vmem,
        scratch_shapes=[
            pltpu.VMEM((n_all * rows, width), jnp.bfloat16),
            pltpu.VMEM((n_all, most, rows), jnp.int32),
            pltpu.VMEM((rows, width), jnp.float32),
            pltpu.VMEM((most, rows, 128), jnp.int32),
            pltpu.SemaphoreType.DMA((n_dp // 2, 4)),
            pltpu.SemaphoreType.DMA((events,)),
            pltpu.SemaphoreType.DMA((events,)),
            pltpu.SemaphoreType.DMA((events,)),
            pltpu.SemaphoreType.DMA((n_all, 2)),
            pltpu.SemaphoreType.DMA,
            pltpu.SemaphoreType.DMA,
        ],
        compiler_params=pltpu.CompilerParams(
            collective_id=0, has_side_effects=True, vmem_limit_bytes=60 * 1024 * 1024
        ),
    )(log_scale, bias, embed, theirs)


def solution(mesh):
    return jax.shard_map(
        functools.partial(body, mesh.shape["blk"], mesh.shape["dp"]),
        mesh=mesh,
        in_specs=(
            P(("blk", "dp"), None),
            P(),
            P(),
            P(("blk", "dp")),
            P(("blk", "dp"), None),
            P(("blk", "dp"), None),
        ),
        out_specs=P(("blk", "dp"), None),
        check_vma=False,
    )
```

```python
import functools
import math

import jax
import jax.numpy as jnp
from jax import lax
from jax.experimental import pallas as pl
from jax.experimental.pallas import tpu as pltpu
from jax.sharding import PartitionSpec as P

MESH = pl.DeviceIdType.MESH


def lookup(table, index):
    value = jnp.int32(table[0])
    for k in range(1, len(table)):
        value = jnp.where(index == k, jnp.int32(table[k]), value)
    return value


def kernel(
    n_blk, n_dp, log_scale_ref, bias_ref, x_ref, theirs_ref, o_ref,
    buf, keys, acc, wanted, z_sem, right_sem, left_sem, sib_sem, recv_sem, key_send, key_recv,
):
    rows, width = x_ref.shape
    most = theirs_ref.shape[1]
    half = rows // 2
    n_all = n_blk * n_dp
    n_z = n_dp // 2
    far = n_blk // 2
    events = n_blk * n_z
    i, j = lax.axis_index("blk"), lax.axis_index("dp")
    z, c = j // 2, j % 2
    me = i * n_dp + j

    ring = [p ^ (p >> 1) for p in range(n_blk)]
    place = [ring.index(k) for k in range(n_blk)]
    pos = lookup(place, i)
    blk_at = lambda p: lookup(ring, lax.rem(p + n_blk, n_blk))
    right, left = blk_at(pos + 1), blk_at(pos - 1)
    order = []
    for a in range(n_z):
        order += sorted(range(n_z), key=lambda b: (abs(b - a), b))
    z_at = lambda t: lookup(order, z * n_z + t)
    slot = lambda bi, zz, cc: (bi * n_z + zz) * 2 + cc

    def copy(f, h, device, send, recv):
        if h is None:
            span = pl.ds(pl.multiple_of(f * rows, rows), rows)
        else:
            span = pl.ds(pl.multiple_of(f * rows + h * half, half), half)
        return pltpu.make_async_remote_copy(
            src_ref=buf.at[span], dst_ref=buf.at[span], send_sem=send, recv_sem=recv,
            device_id=device, device_id_type=MESH,
        )

    def to_right(f, h, e):
        return copy(f, h, (right, j), right_sem.at[e], recv_sem.at[f, h or 0])

    def to_left(f, h, e):
        return copy(f, h, (left, j), left_sem.at[e], recv_sem.at[f, h or 0])

    def to_sib(f, e):
        return copy(f, None, (i, z * 2 + 1 - c), sib_sem.at[e], recv_sem.at[f, 0])

    def along_z(zz, step, k):
        f = slot(i, zz, c)
        return copy(f, None, (i, (z + step) * 2 + c), z_sem.at[zz, k], recv_sem.at[f, 0])

    far_blk = blk_at(pos + far)

    def far_along_z(zz, step, k):
        f = slot(far_blk, zz, c)
        return copy(f, None, (i, (z + step) * 2 + c), z_sem.at[zz, 2 + k], recv_sem.at[f, 0])

    def reach(zz):
        return jnp.where(jnp.logical_and(zz >= 0, zz < n_z), 1, 0)

    def halves(zz):
        return jnp.logical_or(zz == z, jnp.maximum(zz - z, z - zz) > reach(z))

    def arrived(f, h):
        copy(f, h, (right, j), right_sem.at[0], recv_sem.at[f, h or 0]).wait_recv()

    def place_of(e):
        t, m = e // n_blk, e % n_blk
        t = jnp.where(m == n_blk - 1, t - 1, t)
        d = (m + 1) // 2
        return t, m, d, blk_at(jnp.where(m % 2 == 1, pos - d, pos + d)), z_at(t)

    barrier = pltpu.get_barrier_semaphore()

    @pl.loop(1, n_all)
    def _(k):
        f = lax.rem(me + k, n_all)
        pl.semaphore_signal(barrier, 1, device_id=(f // n_dp, f % n_dp), device_id_type=MESH)

    root = 1.0 / math.sqrt(width)
    x = x_ref[...].astype(jnp.float32)
    inv = lax.rsqrt(jnp.mean(x * x, axis=1, keepdims=True) + 1e-06)
    own = pl.ds(pl.multiple_of(me * rows, rows), rows)
    buf[own, :] = (x * inv * root).astype(jnp.bfloat16)
    keys[pl.ds(me, 1)] = theirs_ref[...]
    pl.semaphore_wait(barrier, n_all - 1)

    to_right(me, None, z).start()
    to_left(me, None, z).start()

    @pl.when(z < n_z - 1)
    def _():
        along_z(z, 1, 0).start()

    @pl.when(z > 0)
    def _():
        along_z(z, -1, 1).start()

    to_sib(me, z).start()

    def key_copy(src, dst, f):
        return pltpu.make_async_remote_copy(
            src_ref=src, dst_ref=dst, send_sem=key_send, recv_sem=key_recv,
            device_id=(f // n_dp, f % n_dp), device_id_type=MESH,
        )

    @pl.loop(1, n_all)
    def _(k):
        f = lax.rem(me + k, n_all)
        key_copy(theirs_ref, keys.at[pl.ds(me, 1)], f).start()

    acc[...] = jnp.zeros_like(acc)
    for k in range(most):
        wanted[k] = jnp.broadcast_to(theirs_ref[0, k : k + 1, :], (128, rows)).T
    scale = jnp.exp(jnp.full((1, 1), log_scale_ref[0], jnp.float32))
    offset = jnp.full((1, 1), bias_ref[0], jnp.float32)
    everything = keys.at[pl.ds(0, n_all - 1)]

    def compute(e):
        _, _, _, bi, zz = place_of(e)
        arrived(slot(bi, zz, 1 - c), None)
        pair = bi * n_z + zz
        start = pair * 2 * rows
        block = buf[pl.ds(pl.multiple_of(start, 2 * rows), 2 * rows), :]
        scores = lax.dot_general(
            buf[own, :], block, (((1,), (1,)), ((), ())), preferred_element_type=jnp.float32
        )
        lanes = lax.broadcasted_iota(jnp.int32, (rows, 128), 1)
        here = lax.broadcasted_iota(jnp.int32, (rows, 128), 0) + me * rows
        weights = []
        for u in range(2 * rows // 128):
            side, at = u * 128 // rows, u * 128 % rows
            columns = lanes + (start + u * 128)
            named = jnp.zeros((rows, 128), jnp.float32)
            for k in range(most):
                named += jnp.where(wanted[k] == columns, 1.0, 0.0)
            for k in range(most):
                key = keys[pair * 2 + side, k : k + 1, at : at + 128]
                named += jnp.where(key == here, 1.0, 0.0)
            power = jnp.exp(offset + scale * scores[:, u * 128 : (u + 1) * 128])
            gain = jnp.where(jnp.logical_and(zz == z, c == side), 2.0, 0.0)
            negative = jnp.where(columns == here, 0.0, gain * power)
            weights.append(((negative - named) / (1.0 + power)).astype(jnp.bfloat16))
        weight = jnp.concatenate(weights, axis=1)
        acc[...] += jnp.dot(weight, block, preferred_element_type=jnp.float32)

    @pl.loop(0, events + n_blk)
    def _(e):
        t, m, d, bi, zz = place_of(e)
        valid = jnp.logical_and(t >= 0, t < n_z)

        for step, k in ((1, 1), (-1, 0)):
            origin = z + step * (t + 1)

            @pl.when(jnp.logical_and(m == 0, jnp.logical_and(origin >= 0, origin < n_z)))
            def _():
                f = slot(i, origin, c)
                arrived(f, None)

                @pl.when(jnp.logical_and(z - step >= 0, z - step < n_z))
                def _():
                    along_z(origin, -step, k).start()

                to_right(f, None, origin).start()
                to_left(f, None, origin).start()
                to_sib(f, origin).start()

        passing = jnp.logical_and(valid, jnp.logical_and(m % 2 == 1, m < n_blk - 1))
        for parity, send in ((1, to_right), (0, to_left)):
            f = slot(blk_at(pos - d if parity else pos + d), zz, c)
            index = (2 * d - parity) * n_z + zz

            @pl.when(passing)
            def _():
                arrived(f, None)

            @pl.when(jnp.logical_and(jnp.logical_and(passing, halves(zz)), d == far - 1))
            def _():
                send(f, 1 - parity, index).start()

            if far > 2:
                @pl.when(jnp.logical_and(passing, d < far - 1))
                def _():
                    send(f, None, index).start()

            @pl.when(passing)
            def _():
                to_sib(f, index).start()

        for step, k in ((1, 1), (-1, 0)):
            origin = z + step * t
            here = jnp.logical_and(origin >= 0, origin < n_z)
            here = jnp.logical_and(here, jnp.logical_and(m == n_blk - 1, valid))
            if step < 0:
                here = jnp.logical_and(here, t > 0)

            @pl.when(here)
            def _():
                g = slot(far_blk, origin, c)

                @pl.when(halves(origin))
                def _():
                    arrived(g, 0)
                    arrived(g, 1)

                @pl.when(jnp.logical_not(halves(origin)))
                def _():
                    arrived(g, None)

                @pl.when(t + 1 <= reach(z - step))
                def _():
                    far_along_z(origin, -step, k).start()

                @pl.when(jnp.logical_and(t == 0, 1 <= reach(z + step)))
                def _():
                    far_along_z(origin, step, 1 - k).start()

                to_sib(g, (n_blk - 1) * n_z + origin).start()

        @pl.when(e == 1)
        def _():
            key_copy(everything, everything, lax.rem(me + 1, n_all)).wait()

        before = place_of(e - 1 + n_blk)[0] - 1

        @pl.when(jnp.logical_and(e > 0, jnp.logical_and(before >= 0, before < n_z)))
        def _():
            compute(e - 1)

    compute(events + n_blk - 1)

    t_acc = scale * acc[...]
    x = x_ref[...].astype(jnp.float32)
    inv = lax.rsqrt(jnp.mean(x * x, axis=1, keepdims=True) + 1e-06)
    inner = jnp.sum(x * t_acc, axis=1, keepdims=True)
    o_ref[...] = (root * inv * (t_acc - x * (inv * inv * inner / width))).astype(o_ref.dtype)

    @pl.loop(0, n_z)
    def _(zz):
        @pl.when(jnp.logical_and(zz <= z, z < n_z - 1))
        def _():
            along_z(zz, 1, 0).wait_send()

        @pl.when(jnp.logical_and(zz >= z, z > 0))
        def _():
            along_z(zz, -1, 1).wait_send()

        @pl.when(jnp.logical_and(zz <= z, z + 1 - zz <= reach(z + 1)))
        def _():
            far_along_z(zz, 1, 0).wait_send()

        @pl.when(jnp.logical_and(zz >= z, zz - z + 1 <= reach(z - 1)))
        def _():
            far_along_z(zz, -1, 1).wait_send()

    @pl.loop(0, events)
    def _(e):
        m, zz = e // n_z, e % n_z
        to_sib(me, e).wait_send()

        @pl.when(m == 0)
        def _():
            to_right(me, None, e).wait_send()
            to_left(me, None, e).wait_send()

        passing = jnp.logical_and(m > 0, m < n_blk - 1)
        for parity, send in ((1, to_right), (0, to_left)):
            mine = jnp.logical_and(passing, m % 2 == parity)

            @pl.when(jnp.logical_and(jnp.logical_and(mine, halves(zz)), (m + 1) // 2 == far - 1))
            def _():
                send(me, 0, e).wait_send()

            if far > 2:
                @pl.when(jnp.logical_and(mine, (m + 1) // 2 < far - 1))
                def _():
                    send(me, None, e).wait_send()


def plane_kernel(
    log_scale_hbm, bias_hbm, x_hbm, count_hbm, owner_hbm, row_hbm, o_ref,
    log_scale_ref, bias_ref, x_ref, count_ref, owner_ref, row_ref, grp, col, grp_keys, col_keys, wanted, here, acc, back, out_sums, in_sums, mine_back, their_back, far_back,
    send_sem, recv_sem, load_sem,
):
    rows, width = x_ref.shape
    most = owner_ref.shape[0]
    loads = []
    for source, target in (
        (x_hbm, x_ref), (count_hbm, count_ref), (owner_hbm, owner_ref), (row_hbm, row_ref),
        (log_scale_hbm, log_scale_ref), (bias_hbm, bias_ref),
    ):
        loads.append(pltpu.make_async_copy(source, target, load_sem.at[len(loads)]))
        loads[-1].start()
    half = rows // 2
    n_dp = 8
    i, j = lax.axis_index("blk"), lax.axis_index("dp")
    z, c = j // 2, j % 2
    low = z < 2
    mid = jnp.logical_or(z == 1, z == 2)
    end = jnp.logical_not(mid)
    inner = jnp.where(low, z + 1, z - 1)
    outer = jnp.where(low, z - 1, z + 1)
    far = jnp.where(mid, 3 - outer, 3 - z)
    opposite = jnp.where(low, 2, 1)
    blk_of = [i, i + 1 - 2 * (i % 2), (i + 2) % 4, (i + 1 - 2 * (i % 2) + 2) % 4]
    X, Y = (blk_of[1], j), (blk_of[2], j)
    SIB = (i, z * 2 + 1 - c)
    IN, OUT = (i, inner * 2 + c), (i, outer * 2 + c)
    FAR = (i, jnp.where(mid, far, opposite) * 2 + c)
    planes = [z, inner, outer, far]
    first = jnp.where(mid, 3, 1)
    second = jnp.where(mid, 1, 3)

    def copy(src, dst, send, recv, device):
        return pltpu.make_async_remote_copy(
            src_ref=src, dst_ref=dst, send_sem=send_sem.at[send], recv_sem=recv_sem.at[recv],
            device_id=device, device_id_type=MESH,
        )

    def part(ref, slot, lo, size):
        return ref.at[slot, pl.ds(lo, size)]

    def group(slot, h, device, send, recv, source=0):
        return copy(part(grp, source, h * half, half), part(grp, slot, h * half, half), send, recv, device)

    to_x = [group(1, h, X, h, h) for h in range(2)]
    to_y = [group(2, h, Y, 2 + h, 2 + h) for h in range(2)]
    x_on = group(3, 0, Y, 4, 4, 1)
    y_on = group(3, 1, X, 5, 5, 2)
    keys_x = copy(grp_keys.at[0], grp_keys.at[1], 6, 6, X)
    keys_y = copy(grp_keys.at[0], grp_keys.at[2], 7, 7, Y)
    keys_on = copy(grp_keys.at[1], grp_keys.at[3], 8, 8, Y)

    def own_col(slot, h, lo, size, device, send, recv):
        return copy(
            part(grp, 0, h * half + lo, size), col.at[slot, h, c, pl.ds(lo, size)], send, recv, device
        )

    quarter = half // 2
    in_slot = jnp.where(mid, 1, 2)
    in_recv = jnp.where(mid, 9, 12)
    to_in = [own_col(in_slot, h, 0, half, IN, 9 + h, in_recv + h) for h in range(2)]
    in_keys = copy(grp_keys.at[0], col_keys.at[in_slot, c], 11, in_recv + 2, IN)
    to_out = [own_col(1, h, 0, half, OUT, 12 + h, 9 + h) for h in range(2)]
    out_keys = copy(grp_keys.at[0], col_keys.at[1, c], 14, 11, OUT)
    to_far = [own_col(3, 0, 0, half, FAR, 15, 15)]
    to_far += [own_col(3, 1, q * quarter, quarter, FAR, 16 + q, 16 + q) for q in range(2)]
    far_keys = copy(grp_keys.at[0], col_keys.at[3, c], 18, 18, FAR)

    def pass_on(h):
        return copy(col.at[3, h, c], col.at[3, h, c], 19 + h, 19 + h, OUT)

    keys_out = copy(col_keys.at[3, c], col_keys.at[3, c], 21, 21, OUT)

    def sib(p, h):
        return copy(col.at[p, h, c], col.at[p, h, c], 22 + p * 3 + h, 22 + p * 3 + h, SIB)

    def sib_keys(p):
        return copy(col_keys.at[p, c], col_keys.at[p, c], 22 + p * 3 + 2, 22 + p * 3 + 2, SIB)

    diag_x = copy(part(out_sums, 2, 0, half), part(in_sums, 2, 0, half), 34, 34, X)
    diag_y = copy(part(out_sums, 2, half, half), part(in_sums, 2, half, half), 35, 35, Y)
    back_x = [copy(part(out_sums, 0, h * half, half), part(in_sums, 0, h * half, half), 36 + h, 36 + h, X) for h in range(2)]
    back_y = [copy(part(out_sums, 1, h * half, half), part(in_sums, 1, h * half, half), 38 + h, 38 + h, Y) for h in range(2)]
    swap = copy(mine_back.at[1], their_back, 40, 40, SIB)
    home = copy(mine_back.at[0], far_back, 41, 41, FAR)

    barrier = pltpu.get_barrier_semaphore()
    for device in (X, Y, SIB, IN, FAR):
        pl.semaphore_signal(barrier, 1, device_id=device, device_id_type=MESH)

    @pl.when(mid)
    def _():
        pl.semaphore_signal(barrier, 1, device_id=OUT, device_id_type=MESH)

    loads[0].wait()
    root = 1.0 / math.sqrt(width)
    x = x_ref[...].astype(jnp.float32)
    inv = lax.rsqrt(jnp.mean(x * x, axis=1, keepdims=True) + 1e-06)
    unit = (x * inv * root).astype(jnp.bfloat16)
    grp[0] = unit
    for load in loads[1:]:
        load.wait()
    live = lax.broadcasted_iota(jnp.int32, (most, rows), 0) < count_ref[...]
    grp_keys[0] = jnp.where(live, owner_ref[...] * rows + row_ref[...], -1)
    pl.semaphore_wait(barrier, 5 + jnp.where(mid, 1, 0))

    to_x[0].start()
    to_y[1].start()

    @pl.when(mid)
    def _():
        to_out[0].start()

    @pl.when(end)
    def _():
        to_far[0].start()

    for h in range(2):
        col[0, h, c] = unit[h * half : (h + 1) * half]
    col_keys[0, c] = grp_keys[0]
    sib(0, 0).start()
    sib(0, 1).start()
    to_x[1].start()
    to_y[0].start()

    @pl.when(mid)
    def _():
        to_out[1].start()
        out_keys.start()

    @pl.when(end)
    def _():
        to_far[1].start()
        to_far[2].start()
        far_keys.start()

    sib_keys(0).start()
    keys_x.start()
    keys_y.start()

    scale = 0.5 * jnp.exp(jnp.full((1, 1), log_scale_ref[0], jnp.float32))
    offset = 0.5 * jnp.full((1, 1), bias_ref[0], jnp.float32)

    def prepare(slot):
        base = (blk_of[slot] * n_dp + j) * rows
        here[slot] = (lax.broadcasted_iota(jnp.int32, (rows, 128), 0) + base).astype(jnp.int16)
        for k in range(most):
            wanted[slot, k] = jnp.broadcast_to(grp_keys[slot, k : k + 1, :], (128, rows)).T.astype(jnp.int16)

    def run(slots, p, h, negative=False, backward=False):
        if isinstance(p, int):
            plane = planes[p]
        else:
            plane = lookup_plane(p)
        block = col[p, h].reshape(rows, width)
        spans = [(g, 0, rows) if isinstance(g, int) else (g[0], g[1] * half, half) for g in slots]
        scores = [
            lax.dot_general(
                grp[g, lo : lo + size], block, (((1,), (1,)), ((), ())), preferred_element_type=jnp.float32
            )
            for g, lo, size in spans
        ]
        one, zero = jnp.bfloat16(1.0), jnp.bfloat16(0.0)
        weights = []
        for n, (g, lo, size) in enumerate(spans):
            pieces = []
            for u in range(2):
                base = ((i * n_dp) + plane * 2 + u) * rows + h * half
                lanes = lax.broadcasted_iota(jnp.int32, (1, 128), 1) + base
                columns = jnp.broadcast_to(lanes, (size, 128)).astype(jnp.int16)
                named = jnp.zeros((size, 128), jnp.bfloat16)
                for k in range(most):
                    named += jnp.where(wanted[g, k, lo : lo + size] == columns, one, zero)
                for k in range(most):
                    key = col_keys[p, u, k : k + 1, h * half : (h + 1) * half]
                    key = jnp.broadcast_to(key, (size, 128)).astype(jnp.int16)
                    named += jnp.where(key == here[g, lo : lo + size], one, zero)
                t = jnp.tanh(scale * scores[n][:, u * 128 : (u + 1) * 128] + offset)
                w = (t - 1.0).astype(jnp.bfloat16) * named
                if negative:
                    away = (t + 1.0) * jnp.where(c == u, 2.0, 0.0)
                    if g == 0:
                        own = lax.broadcasted_iota(jnp.int32, (size, 128), 0) + lo
                        other = lax.broadcasted_iota(jnp.int32, (size, 128), 1) + h * half
                        away = jnp.where(own == other, 0.0, away)
                    w += away.astype(jnp.bfloat16)
                pieces.append(w)
            weights.append(jnp.concatenate(pieces, axis=1))
        for n, (g, lo, size) in enumerate(spans):
            acc[g, lo : lo + size] += jnp.dot(weights[n], block, preferred_element_type=jnp.float32)
        if backward:
            for n, (g, lo, size) in enumerate(spans):
                back[h] += lax.dot_general(
                    weights[n], grp[g, lo : lo + size], (((0,), (0,)), ((), ())),
                    preferred_element_type=jnp.float32,
                )

    early, late = [(1, 0), (2, 1)], [(1, 1), (2, 0)]

    def lookup_plane(p):
        return jnp.where(p == 1, inner, jnp.where(p == 2, outer, far))

    prepare(0)
    acc[...] = jnp.zeros_like(acc)
    back[...] = jnp.zeros_like(back)
    sib(0, 0).wait_recv()
    sib(0, 1).wait_recv()
    sib_keys(0).wait_recv()
    run([0], 0, 0, negative=True)
    run([0], 0, 1, negative=True)

    to_x[0].wait_recv()
    x_on.start()
    to_y[1].wait_recv()
    y_on.start()

    @pl.when(mid)
    def _():
        to_far[0].wait_recv()
        pass_on(0).start()
        far_keys.wait_recv()
        keys_out.start()

    @pl.when(end)
    def _():
        to_out[0].wait_recv()
        out_keys.wait_recv()

    sib(first, 0).start()
    sib_keys(first).start()
    keys_x.wait_recv()
    keys_on.start()
    keys_y.wait_recv()
    prepare(1)
    prepare(2)
    run(early, 0, 0, negative=True)

    @pl.when(mid)
    def _():
        to_far[1].wait_recv()

    @pl.when(end)
    def _():
        to_far[1].wait_send()

    for h in range(2):
        to_in[h].start()
    in_keys.start()
    run(early, 0, 1, negative=True)
    sib(first, 0).wait_recv()
    sib_keys(first).wait_recv()
    run([0] + early, first, 0, backward=True)

    @pl.when(mid)
    def _():
        to_far[2].wait_recv()
        pass_on(1).start()

    @pl.when(end)
    def _():
        to_out[1].wait_recv()

    sib(first, 1).start()
    to_x[1].wait_recv()
    to_y[0].wait_recv()
    run(late, 0, 0, negative=True)
    run(late, 0, 1, negative=True)
    run(late, first, 0, backward=True)
    keys_on.wait_recv()
    prepare(3)
    sib(first, 1).wait_recv()
    run([0, 1, 2], first, 1, backward=True)

    def arrived(p, h):
        return own_col(p, h, 0, half, IN, 9 + h, (9 if p == 1 else 12) + h)

    def keys_arrived(p):
        return copy(grp_keys.at[0], col_keys.at[p, c], 11, 11 if p == 1 else 14, IN)

    @pl.when(mid)
    def _():
        for p in (1, 2):
            arrived(p, 0).wait_recv()
            sib(p, 0).start()
            keys_arrived(p).wait_recv()
            sib_keys(p).start()

    @pl.when(end)
    def _():
        pass_on(0).wait_recv()
        sib(3, 0).start()
        keys_out.wait_recv()
        sib_keys(3).start()

    x_on.wait_recv()
    y_on.wait_recv()
    run([3], first, 0, backward=True)
    run([3], first, 1, backward=True)

    def diagonal_back():
        out_sums[2] = acc[3].astype(jnp.bfloat16)
        diag_x.start()
        diag_y.start()

    @pl.when(mid)
    def _():
        for h in range(2):
            other = back[h, pl.ds(pl.multiple_of((1 - c) * half, half), half), :]
            mine_back[1, h * half : (h + 1) * half] = other.astype(jnp.bfloat16)
        swap.start()
        for p in (1, 2):
            arrived(p, 1).wait_recv()
            sib(p, 1).start()
        for p in (1, 2):
            sib(p, 0).wait_recv()
            sib_keys(p).wait_recv()
        run([3], 0, 0, negative=True)
        run([3], 0, 1, negative=True)
        run([3], 1, 0)
        run([3], 2, 0)
        swap.wait_recv()
        for h in range(2):
            mine = back[h, pl.ds(pl.multiple_of(c * half, half), half), :]
            both = mine + their_back[h * half : (h + 1) * half].astype(jnp.float32)
            mine_back[0, h * half : (h + 1) * half] = both.astype(jnp.bfloat16)
        home.start()
        for p in (1, 2):
            sib(p, 1).wait_recv()
        run([3], 1, 1)
        run([3], 2, 1)
        diagonal_back()
        for h in range(2):
            run(early, 1, h)
            run(early, 2, h)

    @pl.when(end)
    def _():
        pass_on(1).wait_recv()
        sib(3, 1).start()
        sib(3, 0).wait_recv()
        sib_keys(3).wait_recv()
        run([3], 0, 0, negative=True)
        run([3], 0, 1, negative=True)
        run([3], 3, 0)
        sib(3, 1).wait_recv()
        run([3], 3, 1)
        diagonal_back()
        run(early, 3, 0)
        run(early, 3, 1)

    out_sums[0, :half] = acc[1, :half].astype(jnp.bfloat16)
    back_x[0].start()
    out_sums[1, half:] = acc[2, half:].astype(jnp.bfloat16)
    back_y[1].start()

    @pl.when(mid)
    def _():
        for h in range(2):
            run(late + [0], 1, h)
            run(late + [0], 2, h)

    @pl.when(end)
    def _():
        run(late + [0], 3, 0)
        run(late + [0], 3, 1)

    diag_x.wait_recv()
    out_sums[1, :half] = (acc[2, :half] + in_sums[2, :half].astype(jnp.float32)).astype(jnp.bfloat16)
    back_y[0].start()
    diag_y.wait_recv()
    out_sums[0, half:] = (acc[1, half:] + in_sums[2, half:].astype(jnp.float32)).astype(jnp.bfloat16)
    back_x[1].start()

    back_x[0].wait_recv()
    acc[0, :half] += in_sums[0, :half].astype(jnp.float32)
    back_y[1].wait_recv()
    acc[0, half:] += in_sums[1, half:].astype(jnp.float32)

    @pl.when(end)
    def _():
        home.wait_recv()
        acc[0] += far_back[...].astype(jnp.float32)

    back_y[0].wait_recv()
    o_ref[:half] = scale * (acc[0, :half] + in_sums[1, :half].astype(jnp.float32))
    back_x[1].wait_recv()
    o_ref[half:] = scale * (acc[0, half:] + in_sums[0, half:].astype(jnp.float32))

    for sent in to_x + to_y + to_in + back_x + back_y:
        sent.wait_send()
    for sent in (x_on, y_on, keys_x, keys_y, keys_on, in_keys, diag_x, diag_y):
        sent.wait_send()
    for p in (0, 1, 3):
        for h in range(2):
            sib(p, h).wait_send()
        sib_keys(p).wait_send()

    @pl.when(mid)
    def _():
        for sent in to_out + [out_keys, pass_on(0), pass_on(1), keys_out, sib(2, 0), sib(2, 1), sib_keys(2), swap, home]:
            sent.wait_send()

    @pl.when(end)
    def _():
        for sent in (to_far[0], to_far[2], far_keys):
            sent.wait_send()


def finish_kernel(x_ref, t_acc_ref, o_ref):
    width = x_ref.shape[1]
    root = 1.0 / math.sqrt(width)
    t_acc = t_acc_ref[...]
    x = x_ref[...].astype(jnp.float32)
    inv = lax.rsqrt(jnp.mean(x * x, axis=1, keepdims=True) + 1e-06)
    inner = jnp.sum(x * t_acc, axis=1, keepdims=True)
    o_ref[...] = (root * inv * (t_acc - x * (inv * inv * inner / width))).astype(o_ref.dtype)


def plane_call(embed, log_scale, bias, partner_count, partner_owner, partner_row):
    rows, width = embed.shape
    most = partner_owner.shape[1]
    half = rows // 2
    vmem = pl.BlockSpec(memory_space=pltpu.VMEM)
    hbm = pl.BlockSpec(memory_space=pltpu.HBM)
    t_acc = pl.pallas_call(
        plane_kernel,
        out_shape=jax.ShapeDtypeStruct((rows, width), jnp.float32),
        in_specs=[hbm] * 6,
        out_specs=vmem,
        scratch_shapes=[
            pltpu.SMEM((1,), jnp.float32),
            pltpu.SMEM((1,), jnp.float32),
            pltpu.VMEM((rows, width), embed.dtype),
            pltpu.VMEM((1, rows), jnp.int32),
            pltpu.VMEM((most, rows), jnp.int32),
            pltpu.VMEM((most, rows), jnp.int32),
            pltpu.VMEM((4, rows, width), jnp.bfloat16),
            pltpu.VMEM((4, 2, 2, half, width), jnp.bfloat16),
            pltpu.VMEM((4, most, rows), jnp.int32),
            pltpu.VMEM((4, 2, most, rows), jnp.int32),
            pltpu.VMEM((4, most, rows, 128), jnp.int16),
            pltpu.VMEM((4, rows, 128), jnp.int16),
            pltpu.VMEM((4, rows, width), jnp.float32),
            pltpu.VMEM((2, rows, width), jnp.float32),
            pltpu.VMEM((3, rows, width), jnp.bfloat16),
            pltpu.VMEM((3, rows, width), jnp.bfloat16),
            pltpu.VMEM((2, rows, width), jnp.bfloat16),
            pltpu.VMEM((rows, width), jnp.bfloat16),
            pltpu.VMEM((rows, width), jnp.bfloat16),
            pltpu.SemaphoreType.DMA((42,)),
            pltpu.SemaphoreType.DMA((42,)),
            pltpu.SemaphoreType.DMA((6,)),
        ],
        compiler_params=pltpu.CompilerParams(
            collective_id=0, has_side_effects=True, vmem_limit_bytes=28 * 1024 * 1024
        ),
    )(
        log_scale,
        bias,
        *(
            pltpu.with_memory_space_constraint(a, pltpu.HBM)
            for a in (embed, partner_count.reshape(1, rows), partner_owner.T, partner_row.T)
        ),
    )
    return pl.pallas_call(
        finish_kernel,
        out_shape=jax.ShapeDtypeStruct((rows, width), embed.dtype),
        in_specs=[vmem, vmem],
        out_specs=vmem,
        compiler_params=pltpu.CompilerParams(vmem_limit_bytes=8 * 1024 * 1024),
    )(embed, t_acc)


def body(n_blk, n_dp, embed, log_scale, bias, partner_count, partner_owner, partner_row):
    rows, width = embed.shape
    most = partner_owner.shape[1]
    if (n_blk, n_dp, rows) == (4, 8, 256):
        return plane_call(embed, log_scale, bias, partner_count, partner_owner, partner_row)
    n_all = n_blk * n_dp
    events = n_all // 2
    live = jnp.arange(most, dtype=jnp.int32)[:, None] < partner_count[None, :]
    theirs = jnp.where(live, partner_owner.T * rows + partner_row.T, -1).reshape(1, most, rows)
    vmem = pl.BlockSpec(memory_space=pltpu.VMEM)
    smem = pl.BlockSpec(memory_space=pltpu.SMEM)
    return pl.pallas_call(
        functools.partial(kernel, n_blk, n_dp),
        out_shape=jax.ShapeDtypeStruct((rows, width), embed.dtype),
        in_specs=[smem, smem, vmem, vmem],
        out_specs=vmem,
        scratch_shapes=[
            pltpu.VMEM((n_all * rows, width), jnp.bfloat16),
            pltpu.VMEM((n_all, most, rows), jnp.int32),
            pltpu.VMEM((rows, width), jnp.float32),
            pltpu.VMEM((most, rows, 128), jnp.int32),
            pltpu.SemaphoreType.DMA((n_dp // 2, 4)),
            pltpu.SemaphoreType.DMA((events,)),
            pltpu.SemaphoreType.DMA((events,)),
            pltpu.SemaphoreType.DMA((events,)),
            pltpu.SemaphoreType.DMA((n_all, 2)),
            pltpu.SemaphoreType.DMA,
            pltpu.SemaphoreType.DMA,
        ],
        compiler_params=pltpu.CompilerParams(
            collective_id=0, has_side_effects=True, vmem_limit_bytes=60 * 1024 * 1024
        ),
    )(log_scale, bias, embed, theirs)


def solution(mesh):
    return jax.shard_map(
        functools.partial(body, mesh.shape["blk"], mesh.shape["dp"]),
        mesh=mesh,
        in_specs=(
            P(("blk", "dp"), None),
            P(),
            P(),
            P(("blk", "dp")),
            P(("blk", "dp"), None),
            P(("blk", "dp"), None),
        ),
        out_specs=P(("blk", "dp"), None),
        check_vma=False,
    )
```

```python
import functools
import math

import jax
import jax.numpy as jnp
from jax import lax
from jax.experimental import pallas as pl
from jax.experimental.pallas import tpu as pltpu
from jax.sharding import PartitionSpec as P

MESH = pl.DeviceIdType.MESH


def lookup(table, index):
    value = jnp.int32(table[0])
    for k in range(1, len(table)):
        value = jnp.where(index == k, jnp.int32(table[k]), value)
    return value


def kernel(
    n_blk, n_dp, log_scale_ref, bias_ref, x_ref, theirs_ref, o_ref,
    buf, keys, acc, wanted, z_sem, right_sem, left_sem, sib_sem, recv_sem, key_send, key_recv,
):
    rows, width = x_ref.shape
    most = theirs_ref.shape[1]
    half = rows // 2
    n_all = n_blk * n_dp
    n_z = n_dp // 2
    far = n_blk // 2
    events = n_blk * n_z
    i, j = lax.axis_index("blk"), lax.axis_index("dp")
    z, c = j // 2, j % 2
    me = i * n_dp + j

    ring = [p ^ (p >> 1) for p in range(n_blk)]
    place = [ring.index(k) for k in range(n_blk)]
    pos = lookup(place, i)
    blk_at = lambda p: lookup(ring, lax.rem(p + n_blk, n_blk))
    right, left = blk_at(pos + 1), blk_at(pos - 1)
    order = []
    for a in range(n_z):
        order += sorted(range(n_z), key=lambda b: (abs(b - a), b))
    z_at = lambda t: lookup(order, z * n_z + t)
    slot = lambda bi, zz, cc: (bi * n_z + zz) * 2 + cc

    def copy(f, h, device, send, recv):
        if h is None:
            span = pl.ds(pl.multiple_of(f * rows, rows), rows)
        else:
            span = pl.ds(pl.multiple_of(f * rows + h * half, half), half)
        return pltpu.make_async_remote_copy(
            src_ref=buf.at[span], dst_ref=buf.at[span], send_sem=send, recv_sem=recv,
            device_id=device, device_id_type=MESH,
        )

    def to_right(f, h, e):
        return copy(f, h, (right, j), right_sem.at[e], recv_sem.at[f, h or 0])

    def to_left(f, h, e):
        return copy(f, h, (left, j), left_sem.at[e], recv_sem.at[f, h or 0])

    def to_sib(f, e):
        return copy(f, None, (i, z * 2 + 1 - c), sib_sem.at[e], recv_sem.at[f, 0])

    def along_z(zz, step, k):
        f = slot(i, zz, c)
        return copy(f, None, (i, (z + step) * 2 + c), z_sem.at[zz, k], recv_sem.at[f, 0])

    far_blk = blk_at(pos + far)

    def far_along_z(zz, step, k):
        f = slot(far_blk, zz, c)
        return copy(f, None, (i, (z + step) * 2 + c), z_sem.at[zz, 2 + k], recv_sem.at[f, 0])

    def reach(zz):
        return jnp.where(jnp.logical_and(zz >= 0, zz < n_z), 1, 0)

    def halves(zz):
        return jnp.logical_or(zz == z, jnp.maximum(zz - z, z - zz) > reach(z))

    def arrived(f, h):
        copy(f, h, (right, j), right_sem.at[0], recv_sem.at[f, h or 0]).wait_recv()

    def place_of(e):
        t, m = e // n_blk, e % n_blk
        t = jnp.where(m == n_blk - 1, t - 1, t)
        d = (m + 1) // 2
        return t, m, d, blk_at(jnp.where(m % 2 == 1, pos - d, pos + d)), z_at(t)

    barrier = pltpu.get_barrier_semaphore()

    @pl.loop(1, n_all)
    def _(k):
        f = lax.rem(me + k, n_all)
        pl.semaphore_signal(barrier, 1, device_id=(f // n_dp, f % n_dp), device_id_type=MESH)

    root = 1.0 / math.sqrt(width)
    x = x_ref[...].astype(jnp.float32)
    inv = lax.rsqrt(jnp.mean(x * x, axis=1, keepdims=True) + 1e-06)
    own = pl.ds(pl.multiple_of(me * rows, rows), rows)
    buf[own, :] = (x * inv * root).astype(jnp.bfloat16)
    keys[pl.ds(me, 1)] = theirs_ref[...]
    pl.semaphore_wait(barrier, n_all - 1)

    to_right(me, None, z).start()
    to_left(me, None, z).start()

    @pl.when(z < n_z - 1)
    def _():
        along_z(z, 1, 0).start()

    @pl.when(z > 0)
    def _():
        along_z(z, -1, 1).start()

    to_sib(me, z).start()

    def key_copy(src, dst, f):
        return pltpu.make_async_remote_copy(
            src_ref=src, dst_ref=dst, send_sem=key_send, recv_sem=key_recv,
            device_id=(f // n_dp, f % n_dp), device_id_type=MESH,
        )

    @pl.loop(1, n_all)
    def _(k):
        f = lax.rem(me + k, n_all)
        key_copy(theirs_ref, keys.at[pl.ds(me, 1)], f).start()

    acc[...] = jnp.zeros_like(acc)
    for k in range(most):
        wanted[k] = jnp.broadcast_to(theirs_ref[0, k : k + 1, :], (128, rows)).T
    scale = jnp.exp(jnp.full((1, 1), log_scale_ref[0], jnp.float32))
    offset = jnp.full((1, 1), bias_ref[0], jnp.float32)
    everything = keys.at[pl.ds(0, n_all - 1)]

    def compute(e):
        _, _, _, bi, zz = place_of(e)
        arrived(slot(bi, zz, 1 - c), None)
        pair = bi * n_z + zz
        start = pair * 2 * rows
        block = buf[pl.ds(pl.multiple_of(start, 2 * rows), 2 * rows), :]
        scores = lax.dot_general(
            buf[own, :], block, (((1,), (1,)), ((), ())), preferred_element_type=jnp.float32
        )
        lanes = lax.broadcasted_iota(jnp.int32, (rows, 128), 1)
        here = lax.broadcasted_iota(jnp.int32, (rows, 128), 0) + me * rows
        weights = []
        for u in range(2 * rows // 128):
            side, at = u * 128 // rows, u * 128 % rows
            columns = lanes + (start + u * 128)
            named = jnp.zeros((rows, 128), jnp.float32)
            for k in range(most):
                named += jnp.where(wanted[k] == columns, 1.0, 0.0)
            for k in range(most):
                key = keys[pair * 2 + side, k : k + 1, at : at + 128]
                named += jnp.where(key == here, 1.0, 0.0)
            power = jnp.exp(offset + scale * scores[:, u * 128 : (u + 1) * 128])
            gain = jnp.where(jnp.logical_and(zz == z, c == side), 2.0, 0.0)
            negative = jnp.where(columns == here, 0.0, gain * power)
            weights.append(((negative - named) / (1.0 + power)).astype(jnp.bfloat16))
        weight = jnp.concatenate(weights, axis=1)
        acc[...] += jnp.dot(weight, block, preferred_element_type=jnp.float32)

    @pl.loop(0, events + n_blk)
    def _(e):
        t, m, d, bi, zz = place_of(e)
        valid = jnp.logical_and(t >= 0, t < n_z)

        for step, k in ((1, 1), (-1, 0)):
            origin = z + step * (t + 1)

            @pl.when(jnp.logical_and(m == 0, jnp.logical_and(origin >= 0, origin < n_z)))
            def _():
                f = slot(i, origin, c)
                arrived(f, None)

                @pl.when(jnp.logical_and(z - step >= 0, z - step < n_z))
                def _():
                    along_z(origin, -step, k).start()

                to_right(f, None, origin).start()
                to_left(f, None, origin).start()
                to_sib(f, origin).start()

        passing = jnp.logical_and(valid, jnp.logical_and(m % 2 == 1, m < n_blk - 1))
        for parity, send in ((1, to_right), (0, to_left)):
            f = slot(blk_at(pos - d if parity else pos + d), zz, c)
            index = (2 * d - parity) * n_z + zz

            @pl.when(passing)
            def _():
                arrived(f, None)

            @pl.when(jnp.logical_and(jnp.logical_and(passing, halves(zz)), d == far - 1))
            def _():
                send(f, 1 - parity, index).start()

            if far > 2:
                @pl.when(jnp.logical_and(passing, d < far - 1))
                def _():
                    send(f, None, index).start()

            @pl.when(passing)
            def _():
                to_sib(f, index).start()

        for step, k in ((1, 1), (-1, 0)):
            origin = z + step * t
            here = jnp.logical_and(origin >= 0, origin < n_z)
            here = jnp.logical_and(here, jnp.logical_and(m == n_blk - 1, valid))
            if step < 0:
                here = jnp.logical_and(here, t > 0)

            @pl.when(here)
            def _():
                g = slot(far_blk, origin, c)

                @pl.when(halves(origin))
                def _():
                    arrived(g, 0)
                    arrived(g, 1)

                @pl.when(jnp.logical_not(halves(origin)))
                def _():
                    arrived(g, None)

                @pl.when(t + 1 <= reach(z - step))
                def _():
                    far_along_z(origin, -step, k).start()

                @pl.when(jnp.logical_and(t == 0, 1 <= reach(z + step)))
                def _():
                    far_along_z(origin, step, 1 - k).start()

                to_sib(g, (n_blk - 1) * n_z + origin).start()

        @pl.when(e == 1)
        def _():
            key_copy(everything, everything, lax.rem(me + 1, n_all)).wait()

        before = place_of(e - 1 + n_blk)[0] - 1

        @pl.when(jnp.logical_and(e > 0, jnp.logical_and(before >= 0, before < n_z)))
        def _():
            compute(e - 1)

    compute(events + n_blk - 1)

    t_acc = scale * acc[...]
    x = x_ref[...].astype(jnp.float32)
    inv = lax.rsqrt(jnp.mean(x * x, axis=1, keepdims=True) + 1e-06)
    inner = jnp.sum(x * t_acc, axis=1, keepdims=True)
    o_ref[...] = (root * inv * (t_acc - x * (inv * inv * inner / width))).astype(o_ref.dtype)

    @pl.loop(0, n_z)
    def _(zz):
        @pl.when(jnp.logical_and(zz <= z, z < n_z - 1))
        def _():
            along_z(zz, 1, 0).wait_send()

        @pl.when(jnp.logical_and(zz >= z, z > 0))
        def _():
            along_z(zz, -1, 1).wait_send()

        @pl.when(jnp.logical_and(zz <= z, z + 1 - zz <= reach(z + 1)))
        def _():
            far_along_z(zz, 1, 0).wait_send()

        @pl.when(jnp.logical_and(zz >= z, zz - z + 1 <= reach(z - 1)))
        def _():
            far_along_z(zz, -1, 1).wait_send()

    @pl.loop(0, events)
    def _(e):
        m, zz = e // n_z, e % n_z
        to_sib(me, e).wait_send()

        @pl.when(m == 0)
        def _():
            to_right(me, None, e).wait_send()
            to_left(me, None, e).wait_send()

        passing = jnp.logical_and(m > 0, m < n_blk - 1)
        for parity, send in ((1, to_right), (0, to_left)):
            mine = jnp.logical_and(passing, m % 2 == parity)

            @pl.when(jnp.logical_and(jnp.logical_and(mine, halves(zz)), (m + 1) // 2 == far - 1))
            def _():
                send(me, 0, e).wait_send()

            if far > 2:
                @pl.when(jnp.logical_and(mine, (m + 1) // 2 < far - 1))
                def _():
                    send(me, None, e).wait_send()


def plane_kernel(
    log_scale_hbm, bias_hbm, x_hbm, count_hbm, owner_hbm, row_hbm, o_ref,
    log_scale_ref, bias_ref, x_ref, count_ref, owner_ref, row_ref, grp, col, grp_keys, col_keys, wanted, here, acc, back, out_sums, in_sums, mine_back, their_back, far_back,
    send_sem, recv_sem, load_sem,
):
    rows, width = x_ref.shape
    most = owner_ref.shape[0]
    loads = []
    for source, target in (
        (x_hbm, x_ref), (count_hbm, count_ref), (owner_hbm, owner_ref), (row_hbm, row_ref),
        (log_scale_hbm, log_scale_ref), (bias_hbm, bias_ref),
    ):
        loads.append(pltpu.make_async_copy(source, target, load_sem.at[len(loads)]))
        loads[-1].start()
    half = rows // 2
    n_dp = 8
    i, j = lax.axis_index("blk"), lax.axis_index("dp")
    z, c = j // 2, j % 2
    low = z < 2
    mid = jnp.logical_or(z == 1, z == 2)
    end = jnp.logical_not(mid)
    inner = jnp.where(low, z + 1, z - 1)
    outer = jnp.where(low, z - 1, z + 1)
    far = jnp.where(mid, 3 - outer, 3 - z)
    opposite = jnp.where(low, 2, 1)
    blk_of = [i, i + 1 - 2 * (i % 2), (i + 2) % 4, (i + 1 - 2 * (i % 2) + 2) % 4]
    X, Y = (blk_of[1], j), (blk_of[2], j)
    SIB = (i, z * 2 + 1 - c)
    IN, OUT = (i, inner * 2 + c), (i, outer * 2 + c)
    FAR = (i, jnp.where(mid, far, opposite) * 2 + c)
    planes = [z, inner, outer, far]
    first = jnp.where(mid, 3, 1)
    second = jnp.where(mid, 1, 3)

    def copy(src, dst, send, recv, device):
        return pltpu.make_async_remote_copy(
            src_ref=src, dst_ref=dst, send_sem=send_sem.at[send], recv_sem=recv_sem.at[recv],
            device_id=device, device_id_type=MESH,
        )

    def part(ref, slot, lo, size):
        return ref.at[slot, pl.ds(lo, size)]

    def group(slot, h, device, send, recv, source=0):
        return copy(part(grp, source, h * half, half), part(grp, slot, h * half, half), send, recv, device)

    to_x = [group(1, h, X, h, h) for h in range(2)]
    to_y = [group(2, h, Y, 2 + h, 2 + h) for h in range(2)]
    x_on = group(3, 0, Y, 4, 4, 1)
    y_on = group(3, 1, X, 5, 5, 2)
    keys_x = copy(grp_keys.at[0], grp_keys.at[1], 6, 6, X)
    keys_y = copy(grp_keys.at[0], grp_keys.at[2], 7, 7, Y)
    keys_on = copy(grp_keys.at[1], grp_keys.at[3], 8, 8, Y)

    def own_col(slot, h, lo, size, device, send, recv):
        return copy(
            part(grp, 0, h * half + lo, size), col.at[slot, h, c, pl.ds(lo, size)], send, recv, device
        )

    quarter = half // 2
    in_slot = jnp.where(mid, 1, 2)
    in_recv = jnp.where(mid, 9, 12)
    to_in = [own_col(in_slot, h, 0, half, IN, 9 + h, in_recv + h) for h in range(2)]
    in_keys = copy(grp_keys.at[0], col_keys.at[in_slot, c], 11, in_recv + 2, IN)
    to_out = [own_col(1, h, 0, half, OUT, 12 + h, 9 + h) for h in range(2)]
    out_keys = copy(grp_keys.at[0], col_keys.at[1, c], 14, 11, OUT)
    to_far = [own_col(3, 0, 0, half, FAR, 15, 15)]
    to_far += [own_col(3, 1, q * quarter, quarter, FAR, 16 + q, 16 + q) for q in range(2)]
    far_keys = copy(grp_keys.at[0], col_keys.at[3, c], 18, 18, FAR)

    def pass_on(h):
        return copy(col.at[3, h, c], col.at[3, h, c], 19 + h, 19 + h, OUT)

    keys_out = copy(col_keys.at[3, c], col_keys.at[3, c], 21, 21, OUT)

    def sib(p, h):
        return copy(col.at[p, h, c], col.at[p, h, c], 22 + p * 3 + h, 22 + p * 3 + h, SIB)

    def sib_keys(p):
        return copy(col_keys.at[p, c], col_keys.at[p, c], 22 + p * 3 + 2, 22 + p * 3 + 2, SIB)

    diag_x = copy(part(out_sums, 2, 0, half), part(in_sums, 2, 0, half), 34, 34, X)
    diag_y = copy(part(out_sums, 2, half, half), part(in_sums, 2, half, half), 35, 35, Y)
    back_x = [copy(part(out_sums, 0, h * half, half), part(in_sums, 0, h * half, half), 36 + h, 36 + h, X) for h in range(2)]
    back_y = [copy(part(out_sums, 1, h * half, half), part(in_sums, 1, h * half, half), 38 + h, 38 + h, Y) for h in range(2)]
    swap = copy(mine_back.at[1], their_back, 40, 40, SIB)
    home = copy(mine_back.at[0], far_back, 41, 41, FAR)

    barrier = pltpu.get_barrier_semaphore()
    for device in (X, Y, SIB, IN, FAR):
        pl.semaphore_signal(barrier, 1, device_id=device, device_id_type=MESH)

    @pl.when(mid)
    def _():
        pl.semaphore_signal(barrier, 1, device_id=OUT, device_id_type=MESH)

    loads[0].wait()
    root = 1.0 / math.sqrt(width)
    x = x_ref[...].astype(jnp.float32)
    inv = lax.rsqrt(jnp.mean(x * x, axis=1, keepdims=True) + 1e-06)
    unit = (x * inv * root).astype(jnp.bfloat16)
    grp[0] = unit
    for load in loads[1:]:
        load.wait()
    live = lax.broadcasted_iota(jnp.int32, (most, rows), 0) < count_ref[...]
    grp_keys[0] = jnp.where(live, owner_ref[...] * rows + row_ref[...], -1)
    pl.semaphore_wait(barrier, 5 + jnp.where(mid, 1, 0))

    to_x[0].start()
    to_y[1].start()

    @pl.when(mid)
    def _():
        to_out[0].start()

    @pl.when(end)
    def _():
        to_far[0].start()

    for h in range(2):
        col[0, h, c] = unit[h * half : (h + 1) * half]
    col_keys[0, c] = grp_keys[0]
    sib(0, 0).start()
    sib(0, 1).start()
    to_x[1].start()
    to_y[0].start()

    @pl.when(mid)
    def _():
        to_out[1].start()
        out_keys.start()

    @pl.when(end)
    def _():
        to_far[1].start()
        to_far[2].start()
        far_keys.start()

    sib_keys(0).start()
    keys_x.start()
    keys_y.start()

    scale = 0.5 * jnp.exp(jnp.full((1, 1), log_scale_ref[0], jnp.float32))
    offset = 0.5 * jnp.full((1, 1), bias_ref[0], jnp.float32)

    def prepare(slot):
        base = (blk_of[slot] * n_dp + j) * rows
        here[slot] = (lax.broadcasted_iota(jnp.int32, (rows, 128), 0) + base).astype(jnp.int16)
        for k in range(most):
            wanted[slot, k] = jnp.broadcast_to(grp_keys[slot, k : k + 1, :], (128, rows)).T.astype(jnp.int16)

    def run(slots, p, h, negative=False, backward=False):
        if isinstance(p, int):
            plane = planes[p]
        else:
            plane = lookup_plane(p)
        block = col[p, h].reshape(rows, width)
        spans = [(g, 0, rows) if isinstance(g, int) else (g[0], g[1] * half, half) for g in slots]
        scores = [
            lax.dot_general(
                grp[g, lo : lo + size], block, (((1,), (1,)), ((), ())), preferred_element_type=jnp.float32
            )
            for g, lo, size in spans
        ]
        one, zero = jnp.bfloat16(1.0), jnp.bfloat16(0.0)
        weights = []
        for n, (g, lo, size) in enumerate(spans):
            pieces = []
            for u in range(2):
                base = ((i * n_dp) + plane * 2 + u) * rows + h * half
                lanes = lax.broadcasted_iota(jnp.int32, (1, 128), 1) + base
                columns = jnp.broadcast_to(lanes, (size, 128)).astype(jnp.int16)
                named = jnp.zeros((size, 128), jnp.bfloat16)
                for k in range(most):
                    named += jnp.where(wanted[g, k, lo : lo + size] == columns, one, zero)
                for k in range(most):
                    key = col_keys[p, u, k : k + 1, h * half : (h + 1) * half]
                    key = jnp.broadcast_to(key, (size, 128)).astype(jnp.int16)
                    named += jnp.where(key == here[g, lo : lo + size], one, zero)
                t = jnp.tanh(scale * scores[n][:, u * 128 : (u + 1) * 128] + offset)
                w = (t - 1.0).astype(jnp.bfloat16) * named
                if negative:
                    away = (t + 1.0) * jnp.where(c == u, 2.0, 0.0)
                    if g == 0:
                        own = lax.broadcasted_iota(jnp.int32, (size, 128), 0) + lo
                        other = lax.broadcasted_iota(jnp.int32, (size, 128), 1) + h * half
                        away = jnp.where(own == other, 0.0, away)
                    w += away.astype(jnp.bfloat16)
                pieces.append(w)
            weights.append(jnp.concatenate(pieces, axis=1))
        for n, (g, lo, size) in enumerate(spans):
            acc[g, lo : lo + size] += jnp.dot(weights[n], block, preferred_element_type=jnp.float32)
        if backward:
            for n, (g, lo, size) in enumerate(spans):
                back[h] += lax.dot_general(
                    weights[n], grp[g, lo : lo + size], (((0,), (0,)), ((), ())),
                    preferred_element_type=jnp.float32,
                )

    early, late = [(1, 0), (2, 1)], [(1, 1), (2, 0)]

    def lookup_plane(p):
        return jnp.where(p == 1, inner, jnp.where(p == 2, outer, far))

    prepare(0)
    acc[...] = jnp.zeros_like(acc)
    back[...] = jnp.zeros_like(back)
    sib(0, 0).wait_recv()
    sib(0, 1).wait_recv()
    sib_keys(0).wait_recv()
    run([0], 0, 0, negative=True)
    run([0], 0, 1, negative=True)

    to_x[0].wait_recv()
    x_on.start()
    to_y[1].wait_recv()
    y_on.start()

    @pl.when(mid)
    def _():
        to_far[0].wait_recv()
        pass_on(0).start()
        far_keys.wait_recv()
        keys_out.start()

    @pl.when(end)
    def _():
        to_out[0].wait_recv()
        out_keys.wait_recv()

    sib(first, 0).start()
    sib_keys(first).start()
    keys_x.wait_recv()
    keys_on.start()
    keys_y.wait_recv()
    prepare(1)
    prepare(2)

    @pl.when(mid)
    def _():
        to_far[1].wait_recv()

    @pl.when(end)
    def _():
        to_far[1].wait_send()

    for h in range(2):
        to_in[h].start()
    in_keys.start()
    run(early, 0, 0, negative=True)
    run(early, 0, 1, negative=True)
    sib(first, 0).wait_recv()
    sib_keys(first).wait_recv()
    run([0] + early, first, 0, backward=True)

    @pl.when(mid)
    def _():
        to_far[2].wait_recv()
        pass_on(1).start()

    @pl.when(end)
    def _():
        to_out[1].wait_recv()

    sib(first, 1).start()
    to_x[1].wait_recv()
    to_y[0].wait_recv()
    run(late, 0, 0, negative=True)
    run(late, 0, 1, negative=True)
    run(late, first, 0, backward=True)
    keys_on.wait_recv()
    prepare(3)
    sib(first, 1).wait_recv()
    run([0, 1, 2], first, 1, backward=True)

    def arrived(p, h):
        return own_col(p, h, 0, half, IN, 9 + h, (9 if p == 1 else 12) + h)

    def keys_arrived(p):
        return copy(grp_keys.at[0], col_keys.at[p, c], 11, 11 if p == 1 else 14, IN)

    @pl.when(mid)
    def _():
        for p in (1, 2):
            arrived(p, 0).wait_recv()
            sib(p, 0).start()
            keys_arrived(p).wait_recv()
            sib_keys(p).start()

    @pl.when(end)
    def _():
        pass_on(0).wait_recv()
        sib(3, 0).start()
        keys_out.wait_recv()
        sib_keys(3).start()

    x_on.wait_recv()
    y_on.wait_recv()
    run([3], first, 0, backward=True)
    run([3], first, 1, backward=True)

    def diagonal_back():
        out_sums[2] = acc[3].astype(jnp.bfloat16)
        diag_x.start()
        diag_y.start()

    @pl.when(mid)
    def _():
        for h in range(2):
            other = back[h, pl.ds(pl.multiple_of((1 - c) * half, half), half), :]
            mine_back[1, h * half : (h + 1) * half] = other.astype(jnp.bfloat16)
        swap.start()
        for p in (1, 2):
            arrived(p, 1).wait_recv()
            sib(p, 1).start()
        for p in (1, 2):
            sib(p, 0).wait_recv()
            sib_keys(p).wait_recv()
        run([3], 0, 0, negative=True)
        run([3], 0, 1, negative=True)
        run([3], 1, 0)
        run([3], 2, 0)
        swap.wait_recv()
        for h in range(2):
            mine = back[h, pl.ds(pl.multiple_of(c * half, half), half), :]
            both = mine + their_back[h * half : (h + 1) * half].astype(jnp.float32)
            mine_back[0, h * half : (h + 1) * half] = both.astype(jnp.bfloat16)
        home.start()
        for p in (1, 2):
            sib(p, 1).wait_recv()
        run([3], 1, 1)
        run([3], 2, 1)
        diagonal_back()
        for h in range(2):
            run(early, 1, h)
            run(early, 2, h)

    @pl.when(end)
    def _():
        pass_on(1).wait_recv()
        sib(3, 1).start()
        sib(3, 0).wait_recv()
        sib_keys(3).wait_recv()
        run([3], 0, 0, negative=True)
        run([3], 0, 1, negative=True)
        run([3], 3, 0)
        sib(3, 1).wait_recv()
        run([3], 3, 1)
        diagonal_back()
        run(early, 3, 0)
        run(early, 3, 1)

    out_sums[0, :half] = acc[1, :half].astype(jnp.bfloat16)
    back_x[0].start()
    out_sums[1, half:] = acc[2, half:].astype(jnp.bfloat16)
    back_y[1].start()

    @pl.when(mid)
    def _():
        for h in range(2):
            run(late + [0], 1, h)
            run(late + [0], 2, h)

    @pl.when(end)
    def _():
        run(late + [0], 3, 0)
        run(late + [0], 3, 1)

    diag_x.wait_recv()
    out_sums[1, :half] = (acc[2, :half] + in_sums[2, :half].astype(jnp.float32)).astype(jnp.bfloat16)
    back_y[0].start()
    diag_y.wait_recv()
    out_sums[0, half:] = (acc[1, half:] + in_sums[2, half:].astype(jnp.float32)).astype(jnp.bfloat16)
    back_x[1].start()

    back_x[0].wait_recv()
    acc[0, :half] += in_sums[0, :half].astype(jnp.float32)
    back_y[1].wait_recv()
    acc[0, half:] += in_sums[1, half:].astype(jnp.float32)

    @pl.when(end)
    def _():
        home.wait_recv()
        acc[0] += far_back[...].astype(jnp.float32)

    back_y[0].wait_recv()
    o_ref[:half] = scale * (acc[0, :half] + in_sums[1, :half].astype(jnp.float32))
    back_x[1].wait_recv()
    o_ref[half:] = scale * (acc[0, half:] + in_sums[0, half:].astype(jnp.float32))

    for sent in to_x + to_y + to_in + back_x + back_y:
        sent.wait_send()
    for sent in (x_on, y_on, keys_x, keys_y, keys_on, in_keys, diag_x, diag_y):
        sent.wait_send()
    for p in (0, 1, 3):
        for h in range(2):
            sib(p, h).wait_send()
        sib_keys(p).wait_send()

    @pl.when(mid)
    def _():
        for sent in to_out + [out_keys, pass_on(0), pass_on(1), keys_out, sib(2, 0), sib(2, 1), sib_keys(2), swap, home]:
            sent.wait_send()

    @pl.when(end)
    def _():
        for sent in (to_far[0], to_far[2], far_keys):
            sent.wait_send()


def finish_kernel(x_ref, t_acc_ref, o_ref):
    width = x_ref.shape[1]
    root = 1.0 / math.sqrt(width)
    t_acc = t_acc_ref[...]
    x = x_ref[...].astype(jnp.float32)
    inv = lax.rsqrt(jnp.mean(x * x, axis=1, keepdims=True) + 1e-06)
    inner = jnp.sum(x * t_acc, axis=1, keepdims=True)
    o_ref[...] = (root * inv * (t_acc - x * (inv * inv * inner / width))).astype(o_ref.dtype)


def plane_call(embed, log_scale, bias, partner_count, partner_owner, partner_row):
    rows, width = embed.shape
    most = partner_owner.shape[1]
    half = rows // 2
    vmem = pl.BlockSpec(memory_space=pltpu.VMEM)
    hbm = pl.BlockSpec(memory_space=pltpu.HBM)
    t_acc = pl.pallas_call(
        plane_kernel,
        out_shape=jax.ShapeDtypeStruct((rows, width), jnp.float32),
        in_specs=[hbm] * 6,
        out_specs=vmem,
        scratch_shapes=[
            pltpu.SMEM((1,), jnp.float32),
            pltpu.SMEM((1,), jnp.float32),
            pltpu.VMEM((rows, width), embed.dtype),
            pltpu.VMEM((1, rows), jnp.int32),
            pltpu.VMEM((most, rows), jnp.int32),
            pltpu.VMEM((most, rows), jnp.int32),
            pltpu.VMEM((4, rows, width), jnp.bfloat16),
            pltpu.VMEM((4, 2, 2, half, width), jnp.bfloat16),
            pltpu.VMEM((4, most, rows), jnp.int32),
            pltpu.VMEM((4, 2, most, rows), jnp.int32),
            pltpu.VMEM((4, most, rows, 128), jnp.int16),
            pltpu.VMEM((4, rows, 128), jnp.int16),
            pltpu.VMEM((4, rows, width), jnp.float32),
            pltpu.VMEM((2, rows, width), jnp.float32),
            pltpu.VMEM((3, rows, width), jnp.bfloat16),
            pltpu.VMEM((3, rows, width), jnp.bfloat16),
            pltpu.VMEM((2, rows, width), jnp.bfloat16),
            pltpu.VMEM((rows, width), jnp.bfloat16),
            pltpu.VMEM((rows, width), jnp.bfloat16),
            pltpu.SemaphoreType.DMA((42,)),
            pltpu.SemaphoreType.DMA((42,)),
            pltpu.SemaphoreType.DMA((6,)),
        ],
        compiler_params=pltpu.CompilerParams(
            collective_id=0, has_side_effects=True, vmem_limit_bytes=28 * 1024 * 1024
        ),
    )(
        log_scale,
        bias,
        *(
            pltpu.with_memory_space_constraint(a, pltpu.HBM)
            for a in (embed, partner_count.reshape(1, rows), partner_owner.T, partner_row.T)
        ),
    )
    return pl.pallas_call(
        finish_kernel,
        out_shape=jax.ShapeDtypeStruct((rows, width), embed.dtype),
        in_specs=[vmem, vmem],
        out_specs=vmem,
        compiler_params=pltpu.CompilerParams(vmem_limit_bytes=8 * 1024 * 1024),
    )(embed, t_acc)


def body(n_blk, n_dp, embed, log_scale, bias, partner_count, partner_owner, partner_row):
    rows, width = embed.shape
    most = partner_owner.shape[1]
    if (n_blk, n_dp, rows) == (4, 8, 256):
        return plane_call(embed, log_scale, bias, partner_count, partner_owner, partner_row)
    n_all = n_blk * n_dp
    events = n_all // 2
    live = jnp.arange(most, dtype=jnp.int32)[:, None] < partner_count[None, :]
    theirs = jnp.where(live, partner_owner.T * rows + partner_row.T, -1).reshape(1, most, rows)
    vmem = pl.BlockSpec(memory_space=pltpu.VMEM)
    smem = pl.BlockSpec(memory_space=pltpu.SMEM)
    return pl.pallas_call(
        functools.partial(kernel, n_blk, n_dp),
        out_shape=jax.ShapeDtypeStruct((rows, width), embed.dtype),
        in_specs=[smem, smem, vmem, vmem],
        out_specs=vmem,
        scratch_shapes=[
            pltpu.VMEM((n_all * rows, width), jnp.bfloat16),
            pltpu.VMEM((n_all, most, rows), jnp.int32),
            pltpu.VMEM((rows, width), jnp.float32),
            pltpu.VMEM((most, rows, 128), jnp.int32),
            pltpu.SemaphoreType.DMA((n_dp // 2, 4)),
            pltpu.SemaphoreType.DMA((events,)),
            pltpu.SemaphoreType.DMA((events,)),
            pltpu.SemaphoreType.DMA((events,)),
            pltpu.SemaphoreType.DMA((n_all, 2)),
            pltpu.SemaphoreType.DMA,
            pltpu.SemaphoreType.DMA,
        ],
        compiler_params=pltpu.CompilerParams(
            collective_id=0, has_side_effects=True, vmem_limit_bytes=60 * 1024 * 1024
        ),
    )(log_scale, bias, embed, theirs)


def solution(mesh):
    return jax.shard_map(
        functools.partial(body, mesh.shape["blk"], mesh.shape["dp"]),
        mesh=mesh,
        in_specs=(
            P(("blk", "dp"), None),
            P(),
            P(),
            P(("blk", "dp")),
            P(("blk", "dp"), None),
            P(("blk", "dp"), None),
        ),
        out_specs=P(("blk", "dp"), None),
        check_vma=False,
    )
```

```python
import functools
import math

import jax
import jax.numpy as jnp
from jax import lax
from jax.experimental import pallas as pl
from jax.experimental.pallas import tpu as pltpu
from jax.sharding import PartitionSpec as P

MESH = pl.DeviceIdType.MESH


def lookup(table, index):
    value = jnp.int32(table[0])
    for k in range(1, len(table)):
        value = jnp.where(index == k, jnp.int32(table[k]), value)
    return value


def kernel(
    n_blk, n_dp, log_scale_ref, bias_ref, x_ref, theirs_ref, o_ref,
    buf, keys, acc, wanted, z_sem, right_sem, left_sem, sib_sem, recv_sem, key_send, key_recv,
):
    rows, width = x_ref.shape
    most = theirs_ref.shape[1]
    half = rows // 2
    n_all = n_blk * n_dp
    n_z = n_dp // 2
    far = n_blk // 2
    events = n_blk * n_z
    i, j = lax.axis_index("blk"), lax.axis_index("dp")
    z, c = j // 2, j % 2
    me = i * n_dp + j

    ring = [p ^ (p >> 1) for p in range(n_blk)]
    place = [ring.index(k) for k in range(n_blk)]
    pos = lookup(place, i)
    blk_at = lambda p: lookup(ring, lax.rem(p + n_blk, n_blk))
    right, left = blk_at(pos + 1), blk_at(pos - 1)
    order = []
    for a in range(n_z):
        order += sorted(range(n_z), key=lambda b: (abs(b - a), b))
    z_at = lambda t: lookup(order, z * n_z + t)
    slot = lambda bi, zz, cc: (bi * n_z + zz) * 2 + cc

    def copy(f, h, device, send, recv):
        if h is None:
            span = pl.ds(pl.multiple_of(f * rows, rows), rows)
        else:
            span = pl.ds(pl.multiple_of(f * rows + h * half, half), half)
        return pltpu.make_async_remote_copy(
            src_ref=buf.at[span], dst_ref=buf.at[span], send_sem=send, recv_sem=recv,
            device_id=device, device_id_type=MESH,
        )

    def to_right(f, h, e):
        return copy(f, h, (right, j), right_sem.at[e], recv_sem.at[f, h or 0])

    def to_left(f, h, e):
        return copy(f, h, (left, j), left_sem.at[e], recv_sem.at[f, h or 0])

    def to_sib(f, e):
        return copy(f, None, (i, z * 2 + 1 - c), sib_sem.at[e], recv_sem.at[f, 0])

    def along_z(zz, step, k):
        f = slot(i, zz, c)
        return copy(f, None, (i, (z + step) * 2 + c), z_sem.at[zz, k], recv_sem.at[f, 0])

    far_blk = blk_at(pos + far)

    def far_along_z(zz, step, k):
        f = slot(far_blk, zz, c)
        return copy(f, None, (i, (z + step) * 2 + c), z_sem.at[zz, 2 + k], recv_sem.at[f, 0])

    def reach(zz):
        return jnp.where(jnp.logical_and(zz >= 0, zz < n_z), 1, 0)

    def halves(zz):
        return jnp.logical_or(zz == z, jnp.maximum(zz - z, z - zz) > reach(z))

    def arrived(f, h):
        copy(f, h, (right, j), right_sem.at[0], recv_sem.at[f, h or 0]).wait_recv()

    def place_of(e):
        t, m = e // n_blk, e % n_blk
        t = jnp.where(m == n_blk - 1, t - 1, t)
        d = (m + 1) // 2
        return t, m, d, blk_at(jnp.where(m % 2 == 1, pos - d, pos + d)), z_at(t)

    barrier = pltpu.get_barrier_semaphore()

    @pl.loop(1, n_all)
    def _(k):
        f = lax.rem(me + k, n_all)
        pl.semaphore_signal(barrier, 1, device_id=(f // n_dp, f % n_dp), device_id_type=MESH)

    root = 1.0 / math.sqrt(width)
    x = x_ref[...].astype(jnp.float32)
    inv = lax.rsqrt(jnp.mean(x * x, axis=1, keepdims=True) + 1e-06)
    own = pl.ds(pl.multiple_of(me * rows, rows), rows)
    buf[own, :] = (x * inv * root).astype(jnp.bfloat16)
    keys[pl.ds(me, 1)] = theirs_ref[...]
    pl.semaphore_wait(barrier, n_all - 1)

    to_right(me, None, z).start()
    to_left(me, None, z).start()

    @pl.when(z < n_z - 1)
    def _():
        along_z(z, 1, 0).start()

    @pl.when(z > 0)
    def _():
        along_z(z, -1, 1).start()

    to_sib(me, z).start()

    def key_copy(src, dst, f):
        return pltpu.make_async_remote_copy(
            src_ref=src, dst_ref=dst, send_sem=key_send, recv_sem=key_recv,
            device_id=(f // n_dp, f % n_dp), device_id_type=MESH,
        )

    @pl.loop(1, n_all)
    def _(k):
        f = lax.rem(me + k, n_all)
        key_copy(theirs_ref, keys.at[pl.ds(me, 1)], f).start()

    acc[...] = jnp.zeros_like(acc)
    for k in range(most):
        wanted[k] = jnp.broadcast_to(theirs_ref[0, k : k + 1, :], (128, rows)).T
    scale = jnp.exp(jnp.full((1, 1), log_scale_ref[0], jnp.float32))
    offset = jnp.full((1, 1), bias_ref[0], jnp.float32)
    everything = keys.at[pl.ds(0, n_all - 1)]

    def compute(e):
        _, _, _, bi, zz = place_of(e)
        arrived(slot(bi, zz, 1 - c), None)
        pair = bi * n_z + zz
        start = pair * 2 * rows
        block = buf[pl.ds(pl.multiple_of(start, 2 * rows), 2 * rows), :]
        scores = lax.dot_general(
            buf[own, :], block, (((1,), (1,)), ((), ())), preferred_element_type=jnp.float32
        )
        lanes = lax.broadcasted_iota(jnp.int32, (rows, 128), 1)
        here = lax.broadcasted_iota(jnp.int32, (rows, 128), 0) + me * rows
        weights = []
        for u in range(2 * rows // 128):
            side, at = u * 128 // rows, u * 128 % rows
            columns = lanes + (start + u * 128)
            named = jnp.zeros((rows, 128), jnp.float32)
            for k in range(most):
                named += jnp.where(wanted[k] == columns, 1.0, 0.0)
            for k in range(most):
                key = keys[pair * 2 + side, k : k + 1, at : at + 128]
                named += jnp.where(key == here, 1.0, 0.0)
            power = jnp.exp(offset + scale * scores[:, u * 128 : (u + 1) * 128])
            gain = jnp.where(jnp.logical_and(zz == z, c == side), 2.0, 0.0)
            negative = jnp.where(columns == here, 0.0, gain * power)
            weights.append(((negative - named) / (1.0 + power)).astype(jnp.bfloat16))
        weight = jnp.concatenate(weights, axis=1)
        acc[...] += jnp.dot(weight, block, preferred_element_type=jnp.float32)

    @pl.loop(0, events + n_blk)
    def _(e):
        t, m, d, bi, zz = place_of(e)
        valid = jnp.logical_and(t >= 0, t < n_z)

        for step, k in ((1, 1), (-1, 0)):
            origin = z + step * (t + 1)

            @pl.when(jnp.logical_and(m == 0, jnp.logical_and(origin >= 0, origin < n_z)))
            def _():
                f = slot(i, origin, c)
                arrived(f, None)

                @pl.when(jnp.logical_and(z - step >= 0, z - step < n_z))
                def _():
                    along_z(origin, -step, k).start()

                to_right(f, None, origin).start()
                to_left(f, None, origin).start()
                to_sib(f, origin).start()

        passing = jnp.logical_and(valid, jnp.logical_and(m % 2 == 1, m < n_blk - 1))
        for parity, send in ((1, to_right), (0, to_left)):
            f = slot(blk_at(pos - d if parity else pos + d), zz, c)
            index = (2 * d - parity) * n_z + zz

            @pl.when(passing)
            def _():
                arrived(f, None)

            @pl.when(jnp.logical_and(jnp.logical_and(passing, halves(zz)), d == far - 1))
            def _():
                send(f, 1 - parity, index).start()

            if far > 2:
                @pl.when(jnp.logical_and(passing, d < far - 1))
                def _():
                    send(f, None, index).start()

            @pl.when(passing)
            def _():
                to_sib(f, index).start()

        for step, k in ((1, 1), (-1, 0)):
            origin = z + step * t
            here = jnp.logical_and(origin >= 0, origin < n_z)
            here = jnp.logical_and(here, jnp.logical_and(m == n_blk - 1, valid))
            if step < 0:
                here = jnp.logical_and(here, t > 0)

            @pl.when(here)
            def _():
                g = slot(far_blk, origin, c)

                @pl.when(halves(origin))
                def _():
                    arrived(g, 0)
                    arrived(g, 1)

                @pl.when(jnp.logical_not(halves(origin)))
                def _():
                    arrived(g, None)

                @pl.when(t + 1 <= reach(z - step))
                def _():
                    far_along_z(origin, -step, k).start()

                @pl.when(jnp.logical_and(t == 0, 1 <= reach(z + step)))
                def _():
                    far_along_z(origin, step, 1 - k).start()

                to_sib(g, (n_blk - 1) * n_z + origin).start()

        @pl.when(e == 1)
        def _():
            key_copy(everything, everything, lax.rem(me + 1, n_all)).wait()

        before = place_of(e - 1 + n_blk)[0] - 1

        @pl.when(jnp.logical_and(e > 0, jnp.logical_and(before >= 0, before < n_z)))
        def _():
            compute(e - 1)

    compute(events + n_blk - 1)

    t_acc = scale * acc[...]
    x = x_ref[...].astype(jnp.float32)
    inv = lax.rsqrt(jnp.mean(x * x, axis=1, keepdims=True) + 1e-06)
    inner = jnp.sum(x * t_acc, axis=1, keepdims=True)
    o_ref[...] = (root * inv * (t_acc - x * (inv * inv * inner / width))).astype(o_ref.dtype)

    @pl.loop(0, n_z)
    def _(zz):
        @pl.when(jnp.logical_and(zz <= z, z < n_z - 1))
        def _():
            along_z(zz, 1, 0).wait_send()

        @pl.when(jnp.logical_and(zz >= z, z > 0))
        def _():
            along_z(zz, -1, 1).wait_send()

        @pl.when(jnp.logical_and(zz <= z, z + 1 - zz <= reach(z + 1)))
        def _():
            far_along_z(zz, 1, 0).wait_send()

        @pl.when(jnp.logical_and(zz >= z, zz - z + 1 <= reach(z - 1)))
        def _():
            far_along_z(zz, -1, 1).wait_send()

    @pl.loop(0, events)
    def _(e):
        m, zz = e // n_z, e % n_z
        to_sib(me, e).wait_send()

        @pl.when(m == 0)
        def _():
            to_right(me, None, e).wait_send()
            to_left(me, None, e).wait_send()

        passing = jnp.logical_and(m > 0, m < n_blk - 1)
        for parity, send in ((1, to_right), (0, to_left)):
            mine = jnp.logical_and(passing, m % 2 == parity)

            @pl.when(jnp.logical_and(jnp.logical_and(mine, halves(zz)), (m + 1) // 2 == far - 1))
            def _():
                send(me, 0, e).wait_send()

            if far > 2:
                @pl.when(jnp.logical_and(mine, (m + 1) // 2 < far - 1))
                def _():
                    send(me, None, e).wait_send()


def plane_kernel(
    log_scale_hbm, bias_hbm, x_hbm, count_hbm, owner_hbm, row_hbm, o_ref,
    log_scale_ref, bias_ref, x_ref, count_ref, owner_ref, row_ref, grp, col, grp_keys, col_keys, wanted, here, acc, back, out_sums, in_sums, mine_back, their_back, far_back,
    send_sem, recv_sem, load_sem,
):
    rows, width = x_ref.shape
    most = owner_ref.shape[0]
    loads = []
    for source, target in (
        (x_hbm, x_ref), (count_hbm, count_ref), (owner_hbm, owner_ref), (row_hbm, row_ref),
        (log_scale_hbm, log_scale_ref), (bias_hbm, bias_ref),
    ):
        loads.append(pltpu.make_async_copy(source, target, load_sem.at[len(loads)]))
    half = rows // 2
    n_dp = 8
    i, j = lax.axis_index("blk"), lax.axis_index("dp")
    z, c = j // 2, j % 2
    low = z < 2
    mid = jnp.logical_or(z == 1, z == 2)
    end = jnp.logical_not(mid)
    inner = jnp.where(low, z + 1, z - 1)
    outer = jnp.where(low, z - 1, z + 1)
    far = jnp.where(mid, 3 - outer, 3 - z)
    opposite = jnp.where(low, 2, 1)
    blk_of = [i, i + 1 - 2 * (i % 2), (i + 2) % 4, (i + 1 - 2 * (i % 2) + 2) % 4]
    X, Y = (blk_of[1], j), (blk_of[2], j)
    SIB = (i, z * 2 + 1 - c)
    IN, OUT = (i, inner * 2 + c), (i, outer * 2 + c)
    FAR = (i, jnp.where(mid, far, opposite) * 2 + c)
    planes = [z, inner, outer, far]
    first = jnp.where(mid, 3, 1)
    second = jnp.where(mid, 1, 3)

    def copy(src, dst, send, recv, device):
        return pltpu.make_async_remote_copy(
            src_ref=src, dst_ref=dst, send_sem=send_sem.at[send], recv_sem=recv_sem.at[recv],
            device_id=device, device_id_type=MESH,
        )

    def part(ref, slot, lo, size):
        return ref.at[slot, pl.ds(lo, size)]

    def group(slot, h, device, send, recv, source=0):
        return copy(part(grp, source, h * half, half), part(grp, slot, h * half, half), send, recv, device)

    to_x = [group(1, h, X, h, h) for h in range(2)]
    to_y = [group(2, h, Y, 2 + h, 2 + h) for h in range(2)]
    x_on = group(3, 0, Y, 4, 4, 1)
    y_on = group(3, 1, X, 5, 5, 2)
    keys_x = copy(grp_keys.at[0], grp_keys.at[1], 6, 6, X)
    keys_y = copy(grp_keys.at[0], grp_keys.at[2], 7, 7, Y)
    keys_on = copy(grp_keys.at[1], grp_keys.at[3], 8, 8, Y)

    def own_col(slot, h, lo, size, device, send, recv):
        return copy(
            part(grp, 0, h * half + lo, size), col.at[slot, h, c, pl.ds(lo, size)], send, recv, device
        )

    quarter = half // 2
    in_slot = jnp.where(mid, 1, 2)
    in_recv = jnp.where(mid, 9, 12)
    to_in = [own_col(in_slot, h, 0, half, IN, 9 + h, in_recv + h) for h in range(2)]
    in_keys = copy(grp_keys.at[0], col_keys.at[in_slot, c], 11, in_recv + 2, IN)
    to_out = [own_col(1, h, 0, half, OUT, 12 + h, 9 + h) for h in range(2)]
    out_keys = copy(grp_keys.at[0], col_keys.at[1, c], 14, 11, OUT)
    to_far = [own_col(3, 0, 0, half, FAR, 15, 15)]
    to_far += [own_col(3, 1, q * quarter, quarter, FAR, 16 + q, 16 + q) for q in range(2)]
    far_keys = copy(grp_keys.at[0], col_keys.at[3, c], 18, 18, FAR)

    def pass_on(h):
        return copy(col.at[3, h, c], col.at[3, h, c], 19 + h, 19 + h, OUT)

    keys_out = copy(col_keys.at[3, c], col_keys.at[3, c], 21, 21, OUT)

    def sib(p, h):
        return copy(col.at[p, h, c], col.at[p, h, c], 22 + p * 3 + h, 22 + p * 3 + h, SIB)

    def sib_keys(p):
        return copy(col_keys.at[p, c], col_keys.at[p, c], 22 + p * 3 + 2, 22 + p * 3 + 2, SIB)

    diag_x = copy(part(out_sums, 2, 0, half), part(in_sums, 2, 0, half), 34, 34, X)
    diag_y = copy(part(out_sums, 2, half, half), part(in_sums, 2, half, half), 35, 35, Y)
    back_x = [copy(part(out_sums, 0, h * half, half), part(in_sums, 0, h * half, half), 36 + h, 36 + h, X) for h in range(2)]
    back_y = [copy(part(out_sums, 1, h * half, half), part(in_sums, 1, h * half, half), 38 + h, 38 + h, Y) for h in range(2)]
    swap = copy(mine_back.at[1], their_back, 40, 40, SIB)
    home = copy(mine_back.at[0], far_back, 41, 41, FAR)

    barrier = pltpu.get_barrier_semaphore()
    loads[0].start()
    for device in (FAR, IN, X, Y, SIB):
        pl.semaphore_signal(barrier, 1, device_id=device, device_id_type=MESH)

    @pl.when(mid)
    def _():
        pl.semaphore_signal(barrier, 1, device_id=OUT, device_id_type=MESH)

    for load in loads[1:]:
        load.start()
    loads[0].wait()
    root = 1.0 / math.sqrt(width)
    x = x_ref[...].astype(jnp.float32)
    inv = lax.rsqrt(jnp.mean(x * x, axis=1, keepdims=True) + 1e-06)
    unit = (x * inv * root).astype(jnp.bfloat16)
    grp[0] = unit
    for load in loads[1:]:
        load.wait()
    live = lax.broadcasted_iota(jnp.int32, (most, rows), 0) < count_ref[...]
    grp_keys[0] = jnp.where(live, owner_ref[...] * rows + row_ref[...], -1)
    pl.semaphore_wait(barrier, 5 + jnp.where(mid, 1, 0))

    to_x[0].start()
    to_y[1].start()

    @pl.when(mid)
    def _():
        to_out[0].start()

    @pl.when(end)
    def _():
        to_far[0].start()

    for h in range(2):
        col[0, h, c] = unit[h * half : (h + 1) * half]
    col_keys[0, c] = grp_keys[0]
    sib(0, 0).start()
    sib(0, 1).start()
    to_x[1].start()
    to_y[0].start()

    @pl.when(mid)
    def _():
        to_out[1].start()
        out_keys.start()

    @pl.when(end)
    def _():
        to_far[1].start()
        to_far[2].start()
        far_keys.start()

    sib_keys(0).start()
    keys_x.start()
    keys_y.start()

    scale = 0.5 * jnp.exp(jnp.full((1, 1), log_scale_ref[0], jnp.float32))
    offset = 0.5 * jnp.full((1, 1), bias_ref[0], jnp.float32)

    def prepare(slot):
        base = (blk_of[slot] * n_dp + j) * rows
        here[slot] = (lax.broadcasted_iota(jnp.int32, (rows, 128), 0) + base).astype(jnp.int16)
        for k in range(most):
            wanted[slot, k] = jnp.broadcast_to(grp_keys[slot, k : k + 1, :], (128, rows)).T.astype(jnp.int16)

    def run(slots, p, h, negative=False, backward=False):
        if isinstance(p, int):
            plane = planes[p]
        else:
            plane = lookup_plane(p)
        block = col[p, h].reshape(rows, width)
        spans = [(g, 0, rows) if isinstance(g, int) else (g[0], g[1] * half, half) for g in slots]
        scores = [
            lax.dot_general(
                grp[g, lo : lo + size], block, (((1,), (1,)), ((), ())), preferred_element_type=jnp.float32
            )
            for g, lo, size in spans
        ]
        one, zero = jnp.bfloat16(1.0), jnp.bfloat16(0.0)
        weights = []
        for n, (g, lo, size) in enumerate(spans):
            pieces = []
            for u in range(2):
                base = ((i * n_dp) + plane * 2 + u) * rows + h * half
                lanes = lax.broadcasted_iota(jnp.int32, (1, 128), 1) + base
                columns = jnp.broadcast_to(lanes, (size, 128)).astype(jnp.int16)
                named = jnp.zeros((size, 128), jnp.bfloat16)
                for k in range(most):
                    named += jnp.where(wanted[g, k, lo : lo + size] == columns, one, zero)
                for k in range(most):
                    key = col_keys[p, u, k : k + 1, h * half : (h + 1) * half]
                    key = jnp.broadcast_to(key, (size, 128)).astype(jnp.int16)
                    named += jnp.where(key == here[g, lo : lo + size], one, zero)
                t = jnp.tanh(scale * scores[n][:, u * 128 : (u + 1) * 128] + offset)
                w = (t - 1.0).astype(jnp.bfloat16) * named
                if negative:
                    away = (t + 1.0) * jnp.where(c == u, 2.0, 0.0)
                    if g == 0:
                        own = lax.broadcasted_iota(jnp.int32, (size, 128), 0) + lo
                        other = lax.broadcasted_iota(jnp.int32, (size, 128), 1) + h * half
                        away = jnp.where(own == other, 0.0, away)
                    w += away.astype(jnp.bfloat16)
                pieces.append(w)
            weights.append(jnp.concatenate(pieces, axis=1))
        for n, (g, lo, size) in enumerate(spans):
            acc[g, lo : lo + size] += jnp.dot(weights[n], block, preferred_element_type=jnp.float32)
        if backward:
            for n, (g, lo, size) in enumerate(spans):
                back[h] += lax.dot_general(
                    weights[n], grp[g, lo : lo + size], (((0,), (0,)), ((), ())),
                    preferred_element_type=jnp.float32,
                )

    early, late = [(1, 0), (2, 1)], [(1, 1), (2, 0)]

    def lookup_plane(p):
        return jnp.where(p == 1, inner, jnp.where(p == 2, outer, far))

    prepare(0)
    acc[...] = jnp.zeros_like(acc)
    back[...] = jnp.zeros_like(back)
    sib(0, 0).wait_recv()
    sib(0, 1).wait_recv()
    sib_keys(0).wait_recv()
    run([0], 0, 0, negative=True)
    run([0], 0, 1, negative=True)

    to_x[0].wait_recv()
    x_on.start()
    to_y[1].wait_recv()
    y_on.start()

    @pl.when(mid)
    def _():
        to_far[0].wait_recv()
        pass_on(0).start()
        far_keys.wait_recv()
        keys_out.start()

    @pl.when(end)
    def _():
        to_out[0].wait_recv()
        out_keys.wait_recv()

    sib(first, 0).start()
    sib_keys(first).start()
    for h in range(2):
        to_in[h].start()
    in_keys.start()
    keys_x.wait_recv()
    keys_on.start()
    keys_y.wait_recv()
    prepare(1)
    prepare(2)

    @pl.when(mid)
    def _():
        to_far[1].wait_recv()

    @pl.when(end)
    def _():
        to_far[1].wait_send()

    run(early, 0, 0, negative=True)
    run(early, 0, 1, negative=True)
    sib(first, 0).wait_recv()
    sib_keys(first).wait_recv()
    run([0] + early, first, 0, backward=True)

    @pl.when(mid)
    def _():
        to_far[2].wait_recv()
        pass_on(1).start()

    @pl.when(end)
    def _():
        to_out[1].wait_recv()

    sib(first, 1).start()
    to_x[1].wait_recv()
    to_y[0].wait_recv()
    run(late, 0, 0, negative=True)
    run(late, 0, 1, negative=True)
    run(late, first, 0, backward=True)
    keys_on.wait_recv()
    prepare(3)
    sib(first, 1).wait_recv()
    run([0, 1, 2], first, 1, backward=True)

    def arrived(p, h):
        return own_col(p, h, 0, half, IN, 9 + h, (9 if p == 1 else 12) + h)

    def keys_arrived(p):
        return copy(grp_keys.at[0], col_keys.at[p, c], 11, 11 if p == 1 else 14, IN)

    @pl.when(mid)
    def _():
        for p in (1, 2):
            arrived(p, 0).wait_recv()
            sib(p, 0).start()
            keys_arrived(p).wait_recv()
            sib_keys(p).start()

    @pl.when(end)
    def _():
        pass_on(0).wait_recv()
        sib(3, 0).start()
        keys_out.wait_recv()
        sib_keys(3).start()

    x_on.wait_recv()
    y_on.wait_recv()
    run([3], first, 0, backward=True)
    run([3], first, 1, backward=True)

    def diagonal_back():
        out_sums[2, :half] = acc[3, :half].astype(jnp.bfloat16)
        diag_x.start()
        out_sums[2, half:] = acc[3, half:].astype(jnp.bfloat16)
        diag_y.start()

    @pl.when(mid)
    def _():
        for h in range(2):
            other = back[h, pl.ds(pl.multiple_of((1 - c) * half, half), half), :]
            mine_back[1, h * half : (h + 1) * half] = other.astype(jnp.bfloat16)
        swap.start()
        for p in (1, 2):
            arrived(p, 1).wait_recv()
            sib(p, 1).start()
        for p in (1, 2):
            sib(p, 0).wait_recv()
            sib_keys(p).wait_recv()
        run([3], 0, 0, negative=True)
        run([3], 0, 1, negative=True)
        run([3], 1, 0)
        run([3], 2, 0)
        for p in (1, 2):
            sib(p, 1).wait_recv()
        run([3], 1, 1)
        run([3], 2, 1)
        diagonal_back()
        swap.wait_recv()
        for h in range(2):
            mine = back[h, pl.ds(pl.multiple_of(c * half, half), half), :]
            both = mine + their_back[h * half : (h + 1) * half].astype(jnp.float32)
            mine_back[0, h * half : (h + 1) * half] = both.astype(jnp.bfloat16)
        home.start()
        for h in range(2):
            run(early, 1, h)
            run(early, 2, h)

    @pl.when(end)
    def _():
        pass_on(1).wait_recv()
        sib(3, 1).start()
        sib(3, 0).wait_recv()
        sib_keys(3).wait_recv()
        run([3], 0, 0, negative=True)
        run([3], 0, 1, negative=True)
        run([3], 3, 0)
        sib(3, 1).wait_recv()
        run([3], 3, 1)
        diagonal_back()
        run(early, 3, 0)
        run(early, 3, 1)

    out_sums[0, :half] = acc[1, :half].astype(jnp.bfloat16)
    back_x[0].start()
    out_sums[1, half:] = acc[2, half:].astype(jnp.bfloat16)
    back_y[1].start()

    @pl.when(mid)
    def _():
        for h in range(2):
            run(late + [0], 1, h)
            run(late + [0], 2, h)

    @pl.when(end)
    def _():
        run(late + [0], 3, 0)
        run(late + [0], 3, 1)

    diag_x.wait_recv()
    out_sums[1, :half] = (acc[2, :half] + in_sums[2, :half].astype(jnp.float32)).astype(jnp.bfloat16)
    back_y[0].start()
    diag_y.wait_recv()
    out_sums[0, half:] = (acc[1, half:] + in_sums[2, half:].astype(jnp.float32)).astype(jnp.bfloat16)
    back_x[1].start()

    back_x[0].wait_recv()
    acc[0, :half] += in_sums[0, :half].astype(jnp.float32)
    back_y[1].wait_recv()
    acc[0, half:] += in_sums[1, half:].astype(jnp.float32)

    @pl.when(end)
    def _():
        home.wait_recv()
        acc[0] += far_back[...].astype(jnp.float32)

    back_y[0].wait_recv()
    o_ref[:half] = scale * (acc[0, :half] + in_sums[1, :half].astype(jnp.float32))
    back_x[1].wait_recv()
    o_ref[half:] = scale * (acc[0, half:] + in_sums[0, half:].astype(jnp.float32))

    for sent in to_x + to_y + to_in + back_x + back_y:
        sent.wait_send()
    for sent in (x_on, y_on, keys_x, keys_y, keys_on, in_keys, diag_x, diag_y):
        sent.wait_send()
    for p in (0, 1, 3):
        for h in range(2):
            sib(p, h).wait_send()
        sib_keys(p).wait_send()

    @pl.when(mid)
    def _():
        for sent in to_out + [out_keys, pass_on(0), pass_on(1), keys_out, sib(2, 0), sib(2, 1), sib_keys(2), swap, home]:
            sent.wait_send()

    @pl.when(end)
    def _():
        for sent in (to_far[0], to_far[2], far_keys):
            sent.wait_send()


def finish_kernel(x_ref, t_acc_ref, o_ref):
    width = x_ref.shape[1]
    root = 1.0 / math.sqrt(width)
    t_acc = t_acc_ref[...]
    x = x_ref[...].astype(jnp.float32)
    inv = lax.rsqrt(jnp.mean(x * x, axis=1, keepdims=True) + 1e-06)
    inner = jnp.sum(x * t_acc, axis=1, keepdims=True)
    o_ref[...] = (root * inv * (t_acc - x * (inv * inv * inner / width))).astype(o_ref.dtype)


def plane_call(embed, log_scale, bias, partner_count, partner_owner, partner_row):
    rows, width = embed.shape
    most = partner_owner.shape[1]
    half = rows // 2
    vmem = pl.BlockSpec(memory_space=pltpu.VMEM)
    hbm = pl.BlockSpec(memory_space=pltpu.HBM)
    t_acc = pl.pallas_call(
        plane_kernel,
        out_shape=jax.ShapeDtypeStruct((rows, width), jnp.float32),
        in_specs=[hbm] * 6,
        out_specs=vmem,
        scratch_shapes=[
            pltpu.SMEM((1,), jnp.float32),
            pltpu.SMEM((1,), jnp.float32),
            pltpu.VMEM((rows, width), embed.dtype),
            pltpu.VMEM((1, rows), jnp.int32),
            pltpu.VMEM((most, rows), jnp.int32),
            pltpu.VMEM((most, rows), jnp.int32),
            pltpu.VMEM((4, rows, width), jnp.bfloat16),
            pltpu.VMEM((4, 2, 2, half, width), jnp.bfloat16),
            pltpu.VMEM((4, most, rows), jnp.int32),
            pltpu.VMEM((4, 2, most, rows), jnp.int32),
            pltpu.VMEM((4, most, rows, 128), jnp.int16),
            pltpu.VMEM((4, rows, 128), jnp.int16),
            pltpu.VMEM((4, rows, width), jnp.float32),
            pltpu.VMEM((2, rows, width), jnp.float32),
            pltpu.VMEM((3, rows, width), jnp.bfloat16),
            pltpu.VMEM((3, rows, width), jnp.bfloat16),
            pltpu.VMEM((2, rows, width), jnp.bfloat16),
            pltpu.VMEM((rows, width), jnp.bfloat16),
            pltpu.VMEM((rows, width), jnp.bfloat16),
            pltpu.SemaphoreType.DMA((42,)),
            pltpu.SemaphoreType.DMA((42,)),
            pltpu.SemaphoreType.DMA((6,)),
        ],
        compiler_params=pltpu.CompilerParams(
            collective_id=0, has_side_effects=True, vmem_limit_bytes=28 * 1024 * 1024
        ),
    )(
        log_scale,
        bias,
        *(
            pltpu.with_memory_space_constraint(a, pltpu.HBM)
            for a in (embed, partner_count.reshape(1, rows), partner_owner.T, partner_row.T)
        ),
    )
    return pl.pallas_call(
        finish_kernel,
        out_shape=jax.ShapeDtypeStruct((rows, width), embed.dtype),
        in_specs=[vmem, vmem],
        out_specs=vmem,
        compiler_params=pltpu.CompilerParams(vmem_limit_bytes=8 * 1024 * 1024),
    )(embed, t_acc)


def body(n_blk, n_dp, embed, log_scale, bias, partner_count, partner_owner, partner_row):
    rows, width = embed.shape
    most = partner_owner.shape[1]
    if (n_blk, n_dp, rows) == (4, 8, 256):
        return plane_call(embed, log_scale, bias, partner_count, partner_owner, partner_row)
    n_all = n_blk * n_dp
    events = n_all // 2
    live = jnp.arange(most, dtype=jnp.int32)[:, None] < partner_count[None, :]
    theirs = jnp.where(live, partner_owner.T * rows + partner_row.T, -1).reshape(1, most, rows)
    vmem = pl.BlockSpec(memory_space=pltpu.VMEM)
    smem = pl.BlockSpec(memory_space=pltpu.SMEM)
    return pl.pallas_call(
        functools.partial(kernel, n_blk, n_dp),
        out_shape=jax.ShapeDtypeStruct((rows, width), embed.dtype),
        in_specs=[smem, smem, vmem, vmem],
        out_specs=vmem,
        scratch_shapes=[
            pltpu.VMEM((n_all * rows, width), jnp.bfloat16),
            pltpu.VMEM((n_all, most, rows), jnp.int32),
            pltpu.VMEM((rows, width), jnp.float32),
            pltpu.VMEM((most, rows, 128), jnp.int32),
            pltpu.SemaphoreType.DMA((n_dp // 2, 4)),
            pltpu.SemaphoreType.DMA((events,)),
            pltpu.SemaphoreType.DMA((events,)),
            pltpu.SemaphoreType.DMA((events,)),
            pltpu.SemaphoreType.DMA((n_all, 2)),
            pltpu.SemaphoreType.DMA,
            pltpu.SemaphoreType.DMA,
        ],
        compiler_params=pltpu.CompilerParams(
            collective_id=0, has_side_effects=True, vmem_limit_bytes=60 * 1024 * 1024
        ),
    )(log_scale, bias, embed, theirs)


def solution(mesh):
    return jax.shard_map(
        functools.partial(body, mesh.shape["blk"], mesh.shape["dp"]),
        mesh=mesh,
        in_specs=(
            P(("blk", "dp"), None),
            P(),
            P(),
            P(("blk", "dp")),
            P(("blk", "dp"), None),
            P(("blk", "dp"), None),
        ),
        out_specs=P(("blk", "dp"), None),
        check_vma=False,
    )
```
